128 devices in a mesh: row: 8 (over z_hi, x), tensor: 16 (over z_lo, y, core).
Axes of the slice: x: 4, y: 4, z: 4 (z_hi: 2, z_lo: 2; z = z_hi * 2 + z_lo), core: 2. Of those that a mesh axis runs over, the one named last changes fastest.
Arguments:
- cells: bfloat16 [1024, 4, 4096], P(('row', 'tensor')), may hold values from -6 to 6
- norm1_gain: float32 [4096], replicated, may hold values from 0.25 to 1.75
- w_qkv: bfloat16 [4096, 3, 4096], P(None, None, 'tensor'), may hold values from -0.09375 to 0.09375
- row_bias: float32 [32, 1024, 1024], P('tensor', 'row'), may hold values from -12 to 400
- w_out: bfloat16 [4096, 4096], P('tensor'), may hold values from -0.09375 to 0.09375
- norm2_gain: float32 [4096], replicated, may hold values from 0.25 to 1.75
- w_gate_up: bfloat16 [4096, 2, 11008], P(None, None, 'tensor'), may hold values from -0.09375 to 0.09375
- w_down: bfloat16 [11008, 4096], P('tensor'), may hold values from -0.0546875 to 0.0546875
Outputs:
- state: bfloat16 [1024, 4, 4096], P(('row', 'tensor'))
- result: bfloat16 [1024, 4, 4096], P(('row', 'tensor'))
The draws below stay inside these ranges and needn't reach their ends.
All inputs are finite; a program needn't handle non-finite values.
Results may differ from the reference program's by a relative error of at most 0.029.
Values may be sent and summed in bfloat16 or wider, within the bound.
A program may use at most 128 MiB of HBM per device.

```python
import math
import jax
import jax.numpy as jnp
from jax import lax

D = 4096
HEADS = 32
HD = 128
FF = 11008
COLS = 4
ROWS = 1024
N_TENSOR = 16


def draw_row_bias(key, part):
    key_base = jax.random.fold_in(key, 0)
    normal_part = jnp.clip(jax.random.normal(key_base, (HEADS, ROWS, ROWS), jnp.float32), -4.0, 4.0)
    return normal_part.astype(jnp.float32)


def levels(own_key, extent, shards, low, largest):
    level = 1.0
    for dim, shards_of in shards:
        heights = jax.random.uniform(jax.random.fold_in(jax.random.fold_in(own_key, 6), dim), (shards_of,), jnp.float32, low / len(shards), largest / len(shards))
        level = level * jnp.repeat(jnp.exp(heights), extent[dim] // shards_of).reshape((-1,) + (1,) * (len(extent) - 1 - dim))
    return level


def bell_draw(key, dims, deviation, bound, cuts=(), held_as=jnp.bfloat16):
    values = deviation * jax.random.normal(key, dims, jnp.float32)
    if cuts:
        values = values * levels(key, dims, cuts, -0.22, 0.18)
    return jnp.clip(values, -bound, bound).astype(held_as)


def setup_inputs(seed: int = 0) -> dict:
    splits = jax.random.split(jax.random.key(seed), 9)
    cells = bell_draw(splits[0], (ROWS, COLS, D), 1.0, 6.0, ((0, 128),))
    norm1_gain = jnp.clip(1.0 + 0.15 * jax.random.normal(splits[1], (D,), jnp.float32), 0.25, 1.75)
    w_qkv = bell_draw(splits[2], (D, 3, HEADS * HD), D ** -0.5, 0.09375, ((2, 16),))
    row_bias = draw_row_bias(jax.random.fold_in(splits[8], 71), 0)
    w_out = bell_draw(splits[4], (HEADS * HD, D), (HEADS * HD) ** -0.5, 0.09375, ((0, 16),))
    norm2_gain = jnp.clip(1.0 + 0.15 * jax.random.normal(splits[5], (D,), jnp.float32), 0.25, 1.75)
    w_gate_up = bell_draw(splits[6], (D, 2, FF), D ** -0.5, 0.09375, ((2, 16),))
    w_down = bell_draw(splits[7], (FF, D), FF ** -0.5, 0.0546875, ((0, 16),))
    return dict(cells=cells, norm1_gain=norm1_gain, w_qkv=w_qkv, row_bias=row_bias, w_out=w_out, norm2_gain=norm2_gain, w_gate_up=w_gate_up, w_down=w_down)


def normalize(values, gain):
    wide = values.astype(jnp.float32)
    inverse = lax.rsqrt(lax.optimization_barrier(jnp.mean(wide * wide, axis=-1, keepdims=True)) + 1e-05)
    return (wide * inverse * gain).astype(jnp.bfloat16)

def grouped_sum(activated, weight, groups):
    width = activated.shape[-1] // groups
    running = jnp.zeros((activated.shape[0], weight.shape[1]), jnp.float32)
    for group in range(groups):
        part_rows = activated[:, group * width:(group + 1) * width]
        part_weight = weight[group * width:(group + 1) * width]
        partial_sum = jnp.dot(part_rows, part_weight, preferred_element_type=jnp.float32)
        rounded = lax.optimization_barrier(partial_sum.astype(jnp.bfloat16))
        running = running + rounded.astype(jnp.float32)
    return running

def reference(cells, norm1_gain, w_qkv, row_bias, w_out, norm2_gain, w_gate_up, w_down):
    flat_count = ROWS * COLS
    normed = normalize(cells, norm1_gain).reshape(flat_count, D)
    projected = jnp.dot(normed, w_qkv.reshape(D, 3 * HEADS * HD), preferred_element_type=jnp.float32)
    projected = projected.astype(jnp.bfloat16).reshape(ROWS, COLS, 3, HEADS, HD)
    queries = projected[:, :, 0].astype(jnp.float32)
    keys_all = projected[:, :, 1].astype(jnp.float32)
    values_all = projected[:, :, 2].astype(jnp.float32)
    scores = jnp.einsum('ichd,jchd->chij', queries, keys_all) * (1.0 / math.sqrt(HD)) + row_bias[None]
    peak = lax.optimization_barrier(jnp.max(scores, axis=-1, keepdims=True))
    exponent = jnp.exp(scores - peak)
    total = lax.optimization_barrier(jnp.sum(exponent, axis=-1))
    weights = lax.optimization_barrier(exponent.astype(jnp.bfloat16)).astype(jnp.float32)
    summed = jnp.einsum('chij,jchd->ichd', weights, values_all)
    context = (summed / jnp.transpose(total, (2, 0, 1))[..., None]).astype(jnp.bfloat16)
    context = context.reshape(flat_count, HEADS * HD)
    attended = grouped_sum(context, w_out, N_TENSOR)
    state = (cells.astype(jnp.float32).reshape(flat_count, D) + attended).astype(jnp.bfloat16)
    normed_two = normalize(state, norm2_gain)
    gate_up = jnp.dot(normed_two, w_gate_up.reshape(D, 2 * FF), preferred_element_type=jnp.float32)
    gate_up = gate_up.reshape(flat_count, 2, FF)
    activated = (jax.nn.silu(gate_up[:, 0]) * gate_up[:, 1]).astype(jnp.bfloat16)
    feed = grouped_sum(activated, w_down, N_TENSOR)
    result = (state.astype(jnp.float32) + feed).astype(jnp.bfloat16)
    return (state.reshape(ROWS, COLS, D), result.reshape(ROWS, COLS, D))
```

```python
import functools
import math

import jax
import jax.numpy as jnp
from jax import lax
from jax.experimental import pallas as pl
from jax.experimental.pallas import tpu as pltpu
from jax.sharding import PartitionSpec as P

MESH = pl.DeviceIdType.MESH
F32 = jnp.float32
BF16 = jnp.bfloat16
D = 4096
UNITS = 688
UPAD = 768
SCALE = 1.0 / math.sqrt(128)

S_BIAS = 0
S_X = 3
S_ZH = 6
S_CTX = 10
S_AG = 13
AG_YA, AG_YB, AG_YBP, AG_ZA, AG_ZB, AG_CO, AG_C = 13, 16, 19, 22, 26, 27, 28
S_RS = 42
RS_C, RS_ZA, RS_YA, RS_YB, RS_ZB = 42, 50, 54, 57, 63
N_SEM = 64


def rows(start, count):
    return pl.ds(pl.multiple_of(start, 16), count)


def normalize(values, gain):
    wide = values.astype(F32)
    inverse = lax.rsqrt(jnp.mean(wide * wide, axis=-1, keepdims=True) + 1e-05)
    return (wide * inverse * gain).astype(BF16)


def layer(cells, gain1, wqkv_hbm, bias_hbm, wout_hbm, gain2, wgu_hbm, wdown_hbm, state, result,
          wq, wo, wg, wd, G, PT, RC, RZA, RYA, RYB, RZB, BV, QB, XR, ZR, CS, CH, ACT, ssem, rsem, lsem):
    r = lax.axis_index("row")
    t = lax.axis_index("tensor")
    zh, x = r // 4, lax.rem(r, 4)
    k, c = t // 2, lax.rem(t, 2)
    zl, y = k // 4, lax.rem(k, 4)
    head, pair = x // 2, lax.rem(x, 2)

    def m4(v):
        return lax.rem(v + 4, 4)

    def tensor_dev(zl_, y_, c_):
        return (r, zl_ * 8 + y_ * 2 + c_)

    sib = tensor_dev(zl, y, 1 - c)
    zpart = tensor_dev(1 - zl, y, c)
    ydev = {d: tensor_dev(zl, m4(y + d), c) for d in (1, 2, 3)}
    xdev = {d: (zh * 4 + m4(x + d), t) for d in (1, 2, 3)}
    zhpart = ((1 - zh) * 4 + x, t)

    def piece(zl_, y_, c_):
        return c_ * 8 + zl_ * 4 + y_

    def rcopy(src, dst, slot, dev):
        return pltpu.make_async_remote_copy(
            src_ref=src, dst_ref=dst, send_sem=ssem.at[slot], recv_sem=rsem.at[slot],
            device_id=dev, device_id_type=MESH)

    own_bias = pltpu.make_async_copy(bias_hbm.at[head], BV.at[x], lsem.at[0])
    fetch_q = pltpu.make_async_copy(wqkv_hbm, wq, lsem.at[1])
    fetch_o = pltpu.make_async_copy(wout_hbm, wo, lsem.at[2])
    fetch_g = pltpu.make_async_copy(wgu_hbm, wg.at[:, pl.ds(0, UNITS)], lsem.at[3])
    fetch_d = pltpu.make_async_copy(wdown_hbm, wd.at[pl.ds(0, UNITS)], lsem.at[4])
    fetch_q.start()

    barrier = pltpu.get_barrier_semaphore()
    peers = [sib, zpart, zhpart] + [ydev[d] for d in (1, 2, 3)] + [xdev[d] for d in (1, 2, 3)]
    for dev in peers:
        pl.semaphore_signal(barrier, inc=1, device_id=dev, device_id_type=MESH)

    me = piece(zl, y, c)
    for part in range(2):
        G[rows(me * 32 + part * 16, 16), :] = normalize(cells[part * 16:(part + 1) * 16, :], gain1[...])

    pl.semaphore_wait(barrier, len(peers))

    def half(p, h):
        return G.at[rows(p * 32 + h * 16, 16)]

    def gather():
        sends = []

        def send(src, slot, dev):
            cp = rcopy(src, src, slot, dev)
            cp.start()
            sends.append(cp)
            return cp

        zb = send(half(me, 1), AG_ZB, zpart)
        ya = {d: send(half(me, 0), AG_YA + d - 1, ydev[d]) for d in (1, 3, 2)}
        za = {0: send(half(me, 0), AG_ZA, zpart)}
        yb = {d: send(half(me, 1), AG_YB + d - 1, ydev[d]) for d in (1, 3, 2)}
        co = send(G.at[rows(me * 32, 32)], AG_CO, sib)
        count = [0]
        shared = []

        def share(p, h):
            shared.append(send(half(p, h), AG_C + count[0], sib))
            count[0] += 1

        zb.wait_recv()
        other = piece(1 - zl, y, c)
        ybp = {d: send(half(other, 1), AG_YBP + d - 1, ydev[d]) for d in (1, 3, 2)}
        share(other, 1)
        for d in (1, 3, 2):
            ya[d].wait_recv()
            p = piece(zl, m4(y - d), c)
            za[d] = send(half(p, 0), AG_ZA + d, zpart)
            share(p, 0)
        za[0].wait_recv()
        share(other, 0)
        for d in (1, 3, 2):
            yb[d].wait_recv()
            share(piece(zl, m4(y - d), c), 1)
        for d in (1, 3, 2):
            za[d].wait_recv()
            share(piece(1 - zl, m4(y - d), c), 0)
        for d in (1, 3, 2):
            ybp[d].wait_recv()
            share(piece(1 - zl, m4(y - d), c), 1)
        co.wait_recv()
        for cp in shared:
            cp.wait_recv()
        for cp in sends:
            cp.wait_send()

    def scatter(finish):
        sends = []

        def send(src, dst, slot, dev):
            cp = rcopy(src, dst, slot, dev)
            cp.start()
            sends.append(cp)
            return cp

        def zside(zrel):
            return zl if zrel == 0 else 1 - zl

        order = [(1, 1), (1, 3), (1, 2), (1, 0), (0, 1), (0, 3), (0, 2), (0, 0)]
        cs = {}
        for zrel, d in order:
            p = piece(zside(zrel), m4(y + d), 1 - c)
            cs[zrel, d] = send(PT.at[rows(p * 32, 32)], RC.at[zrel * 4 + d], RS_C + zrel * 4 + d, sib)
        za, ya, yb = {}, {}, {}
        for zrel, d in order:
            cs[zrel, d].wait_recv()
            p = piece(zside(zrel), m4(y + d), c)
            slot = RC.at[zrel * 4 + d]
            slot[...] = (slot[...].astype(F32) + PT[rows(p * 32, 32), :].astype(F32)).astype(BF16)
            if zrel == 1:
                za[d] = send(slot.at[pl.ds(0, 16)], RZA.at[d], RS_ZA + d, zpart)
            if d:
                yb[zrel, d] = send(slot.at[pl.ds(16, 16)], RYB.at[zrel, d - 1], RS_YB + zrel * 3 + d - 1, ydev[d])
        for d in (1, 3, 2):
            za[d].wait_recv()
            slot = RC.at[d, pl.ds(0, 16)]
            slot[...] = (slot[...].astype(F32) + RZA[d].astype(F32)).astype(BF16)
            ya[d] = send(slot, RYA.at[d - 1], RS_YA + d - 1, ydev[d])
        total = {}
        for zrel in (1, 0):
            for d in (1, 3, 2):
                yb[zrel, d].wait_recv()
            slot = RC.at[zrel * 4, pl.ds(16, 16)]
            sums = slot[...].astype(F32)
            for d in (1, 2, 3):
                sums = sums + RYB[zrel, d - 1].astype(F32)
            if zrel == 1:
                slot[...] = sums.astype(BF16)
                zb = send(slot, RZB, RS_ZB, zpart)
            else:
                total[1] = sums
        za[0].wait_recv()
        for d in (1, 3, 2):
            ya[d].wait_recv()
        sums = RC[0, 0:16].astype(F32) + RZA[0].astype(F32)
        for d in (1, 2, 3):
            sums = sums + RYA[d - 1].astype(F32)
        finish(0, sums)
        zb.wait_recv()
        finish(1, total[1] + RZB[...].astype(F32))
        for cp in sends:
            cp.wait_send()

    own_bias.start()
    bias_copies = []
    for d in (1, 3, 2):
        cp = rcopy(bias_hbm.at[m4(x + d) // 2], BV.at[x], S_BIAS + d - 1, xdev[d])
        cp.start()
        bias_copies.append(cp)
    gather()
    fetch_q.wait()
    fetch_o.start()
    fetch_g.start()
    fetch_d.start()

    @pl.loop(0, 2)
    def _(m):
        lhs = jnp.concatenate([G[rows(m * 128, 128), :], G[rows(256 + m * 128, 128), :]], axis=0)
        for j in range(3):
            acc = jnp.dot(lhs, wq[j], preferred_element_type=F32).reshape(2, 4, 4, 8, 256)
            for col in range(4):
                both = jnp.concatenate([acc[:1, :, col], acc[1:, :, col]], axis=0)
                tiles = [both[cc, kk] for kk in range(4) for cc in range(2)]
                val = jnp.concatenate(tiles, axis=0).astype(BF16)
                for h in range(2):
                    QB[h, col, rows(m * 64, 64), j * 128:(j + 1) * 128] = val[:, h * 128:(h + 1) * 128]

    xc = {}
    for d in (1, 3, 2):
        peer = m4(x + d)
        xc[d] = rcopy(QB.at[peer // 2, pl.ds(lax.rem(peer, 2) * 2, 2)], XR.at[x], S_X + d - 1, xdev[d])
        xc[d].start()
    own_x = pltpu.make_async_copy(QB.at[head, pl.ds(pair * 2, 2)], XR.at[x], lsem.at[5])
    own_x.start()
    wg[:, UNITS:UPAD, :] = jnp.zeros((2, UPAD - UNITS, D), BF16)
    wd[UNITS:UPAD, :] = jnp.zeros((UPAD - UNITS, D), BF16)
    own_x.wait()
    zc = {}
    for d in (0, 1, 3, 2):
        if d:
            xc[d].wait_recv()
        src = m4(x - d)
        zc[d] = rcopy(XR.at[src, :, :, pl.ds(128, 256)], ZR.at[src], S_ZH + d, zhpart)
        zc[d].start()
    own_bias.wait()
    for cp in bias_copies:
        cp.wait_recv()
    for d in range(4):
        zc[d].wait_recv()

    near, far = pl.multiple_of(zh * 512, 512), pl.multiple_of((1 - zh) * 512, 512)
    ctx = {}
    for d in (1, 3, 2, 0):
        block = m4(x + d)
        heads_out = []
        for col in range(2):
            q = XR[block, col, :, 0:128]
            k1 = XR[:, col, :, 128:256].reshape(512, 128)
            k2 = ZR[:, col, :, 0:128].reshape(512, 128)
            dims = (((1,), (1,)), ((), ()))
            s1 = lax.dot_general(q, k1, dims, preferred_element_type=F32) * SCALE + BV[block, :, pl.ds(near, 512)]
            s2 = lax.dot_general(q, k2, dims, preferred_element_type=F32) * SCALE + BV[block, :, pl.ds(far, 512)]
            peak = jnp.maximum(jnp.max(s1, axis=-1, keepdims=True), jnp.max(s2, axis=-1, keepdims=True))
            e1, e2 = jnp.exp(s1 - peak), jnp.exp(s2 - peak)
            total = jnp.sum(e1, axis=-1, keepdims=True) + jnp.sum(e2, axis=-1, keepdims=True)
            v1 = XR[:, col, :, 256:384].reshape(512, 128)
            v2 = ZR[:, col, :, 128:256].reshape(512, 128)
            out = jnp.dot(e1.astype(BF16), v1, preferred_element_type=F32)
            out = out + jnp.dot(e2.astype(BF16), v2, preferred_element_type=F32)
            heads_out.append((out / total).reshape(8, 2, 8, 128))
        tiles = [heads_out[col][kk, cc] for cc in range(2) for kk in range(8) for col in range(2)]
        CS[block] = jnp.concatenate(tiles, axis=0).astype(BF16).reshape(16, 16, 128)
        if d:
            ctx[d] = rcopy(CS.at[block], CH.at[head, :, pair], S_CTX + d - 1, xdev[d])
        else:
            ctx[d] = pltpu.make_async_copy(CS.at[block], CH.at[head, :, pair], lsem.at[6])
        ctx[d].start()
    fetch_o.wait()
    ctx[0].wait()
    for d in (1, 3, 2):
        ctx[d].wait_recv()

    @pl.loop(0, 8)
    def _(n):
        lhs = jnp.concatenate([CH[0].reshape(512, 128), CH[1].reshape(512, 128)], axis=1)
        span = pl.ds(pl.multiple_of(n * 512, 512), 512)
        PT[:, span] = jnp.dot(lhs, wo[:, span], preferred_element_type=F32).astype(BF16)

    def add_attended(h, sums):
        part = slice(h * 16, (h + 1) * 16)
        state[part, :] = (cells[part, :].astype(F32) + sums).astype(BF16)
        G[rows(me * 32 + h * 16, 16), :] = normalize(state[part, :], gain2[...])

    scatter(add_attended)
    gather()
    fetch_g.wait()
    fetch_d.wait()

    @pl.loop(0, 3)
    def _(n):
        span = rows(n * 256, 256)
        dims = (((1,), (1,)), ((), ()))
        for m in range(2):
            lhs = G[m * 256:(m + 1) * 256, :]
            gate = lax.dot_general(lhs, wg[0, span, :], dims, preferred_element_type=F32)
            up = lax.dot_general(lhs, wg[1, span, :], dims, preferred_element_type=F32)
            ACT[m * 256:(m + 1) * 256, pl.ds(pl.multiple_of(n * 256, 256), 256)] = (
                gate / (1.0 + jnp.exp(-gate)) * up).astype(BF16)

    @pl.loop(0, 8)
    def _(n):
        span = pl.ds(pl.multiple_of(n * 512, 512), 512)
        PT[:, span] = jnp.dot(ACT[...], wd[:, span], preferred_element_type=F32).astype(BF16)

    def add_feed(h, sums):
        part = slice(h * 16, (h + 1) * 16)
        result[part, :] = (state[part, :].astype(F32) + sums).astype(BF16)

    scatter(add_feed)
    for cp in bias_copies:
        cp.wait_send()
    for d in (1, 2, 3):
        xc[d].wait_send()
        ctx[d].wait_send()
    for d in range(4):
        zc[d].wait_send()


def shards(cells, norm1_gain, w_qkv, row_bias, w_out, norm2_gain, w_gate_up, w_down):
    own = cells.transpose(1, 0, 2).reshape(32, D)
    vmem = pl.BlockSpec(memory_space=pltpu.VMEM)
    hbm = pl.BlockSpec(memory_space=pl.ANY)
    out = jax.ShapeDtypeStruct((32, D), BF16)
    state, result = pl.pallas_call(
        layer,
        out_shape=(out, out),
        in_specs=[vmem, vmem, hbm, hbm, hbm, vmem, hbm, hbm],
        out_specs=(vmem, vmem),
        scratch_shapes=[
            pltpu.VMEM((3, D, 256), BF16),
            pltpu.VMEM((256, D), BF16),
            pltpu.VMEM((2, UPAD, D), BF16),
            pltpu.VMEM((UPAD, D), BF16),
            pltpu.VMEM((512, D), BF16),
            pltpu.VMEM((512, D), BF16),
            pltpu.VMEM((8, 32, D), BF16),
            pltpu.VMEM((4, 16, D), BF16),
            pltpu.VMEM((3, 16, D), BF16),
            pltpu.VMEM((2, 3, 16, D), BF16),
            pltpu.VMEM((16, D), BF16),
            pltpu.VMEM((4, 128, 1024), F32),
            pltpu.VMEM((2, 4, 128, 384), BF16),
            pltpu.VMEM((4, 2, 128, 384), BF16),
            pltpu.VMEM((4, 2, 128, 256), BF16),
            pltpu.VMEM((4, 16, 16, 128), BF16),
            pltpu.VMEM((2, 16, 2, 16, 128), BF16),
            pltpu.VMEM((512, UPAD), BF16),
            pltpu.SemaphoreType.DMA((N_SEM,)),
            pltpu.SemaphoreType.DMA((N_SEM,)),
            pltpu.SemaphoreType.DMA((8,)),
        ],
        compiler_params=pltpu.CompilerParams(
            collective_id=0, has_side_effects=True, vmem_limit_bytes=60 * 2**20),
        name="layer",
    )(own, norm1_gain.reshape(1, D), w_qkv.transpose(1, 0, 2), row_bias, w_out,
      norm2_gain.reshape(1, D), w_gate_up.transpose(1, 2, 0), w_down)
    return tuple(v.reshape(4, 8, D).transpose(1, 0, 2) for v in (state, result))


def solution(mesh):
    in_specs = (
        P(("row", "tensor"), None, None),
        P(),
        P(None, None, "tensor"),
        P("tensor", "row", None),
        P("tensor", None),
        P(),
        P(None, None, "tensor"),
        P("tensor", None),
    )
    out_specs = (P(("row", "tensor"), None, None), P(("row", "tensor"), None, None))
    return jax.shard_map(shards, mesh=mesh, in_specs=in_specs, out_specs=out_specs, check_vma=False)
```

```python
import functools
import math

import jax
import jax.numpy as jnp
from jax import lax
from jax.experimental import pallas as pl
from jax.experimental.pallas import tpu as pltpu
from jax.sharding import PartitionSpec as P

MESH = pl.DeviceIdType.MESH
F32 = jnp.float32
BF16 = jnp.bfloat16
D = 4096
UNITS = 688
UPAD = 768
SCALE = 1.0 / math.sqrt(128)

S_BIAS, S_X, S_ZH, S_ZQ, S_CTX = 0, 3, 9, 17, 21
AG_Z, AG_Y, AG_FWD, AG_OWN, AG_NEAR, AG_FAR = 29, 39, 43, 47, 49, 57
RS_C, RS_Z, RS_Y, RS_FWD = 67, 83, 91, 95
N_SEM = 99


def rows(start, count):
    return pl.ds(pl.multiple_of(start, 16), count)


def normalize(values, gain):
    wide = values.astype(F32)
    inverse = lax.rsqrt(jnp.mean(wide * wide, axis=-1, keepdims=True) + 1e-05)
    return (wide * inverse * gain).astype(BF16)


def layer(cells, gain1, wqkv_hbm, bias_hbm, wout_hbm, gain2, wgu_hbm, wdown_hbm, state, result,
          wq, wo, wg, wd, G, PT, RC, RZ, RY, RF, BV, QB, XR, CS, CH, ACT, ssem, rsem, lsem):
    r = lax.axis_index("row")
    t = lax.axis_index("tensor")
    zh, x = r // 4, lax.rem(r, 4)
    k, c = t // 2, lax.rem(t, 2)
    zl, y = k // 4, lax.rem(k, 4)

    def m4(v):
        return lax.rem(v + 4, 4)

    def role(x_):
        turn = m4(x_ + c)
        return turn // 2, lax.rem(turn, 2)

    head, pair = role(x)

    def dev(zh_=zh, x_=x, zl_=zl, y_=y, c_=c):
        return (zh_ * 4 + x_, zl_ * 8 + y_ * 2 + c_)

    sib = dev(c_=1 - c)
    zdev = (dev(zl_=1 - zl), dev(zh_=1 - zh, zl_=1 - zl))
    ydev = {d: dev(y_=m4(y + d)) for d in (1, 2, 3)}
    xdev = {d: dev(x_=m4(x + d)) for d in (1, 2, 3)}
    zhpart = dev(zh_=1 - zh)

    def piece(ref, zl_, h, c_, y_):
        return ref.at[rows((zl_ * 16 + h * 8 + c_ * 4 + y_) * 16, 16)]

    def rcopy(src, dst, slot, target):
        return pltpu.make_async_remote_copy(
            src_ref=src, dst_ref=dst, send_sem=ssem.at[slot], recv_sem=rsem.at[slot],
            device_id=target, device_id_type=MESH)

    def fetch(pairs, slot):
        return [pltpu.make_async_copy(src, dst, lsem.at[slot + i]) for i, (src, dst) in enumerate(pairs)]

    own_bias = pltpu.make_async_copy(bias_hbm.at[head], BV.at[x], lsem.at[0])
    fetch_q = fetch([(wqkv_hbm.at[j, pl.ds(i * 1024, 1024)], wq.at[j, pl.ds(i * 1024, 1024)])
                     for j in range(3) for i in range(4)], 8)
    fetch_o = fetch([(wout_hbm.at[pl.ds(i * 64, 64)], wo.at[pl.ds(i * 64, 64)]) for i in range(4)], 20)
    fetch_g = fetch([(wgu_hbm.at[j, pl.ds(i * 176, w)], wg.at[j, pl.ds(i * 176, w)])
                     for i, w in enumerate((176, 176, 176, 160)) for j in range(2)], 24)
    fetch_d = fetch([(wdown_hbm.at[pl.ds(i * 176, w)], wd.at[pl.ds(i * 176, w)])
                     for i, w in enumerate((176, 176, 176, 160))], 32)

    def start(copies):
        for cp in copies:
            cp.start()

    def wait(copies):
        for cp in copies:
            cp.wait()

    start(fetch_q)

    barrier = pltpu.get_barrier_semaphore()
    peers = [sib, zdev[0], zdev[1], zhpart] + [ydev[d] for d in (1, 2, 3)] + [xdev[d] for d in (1, 2, 3)]
    peers += [dev(zh_=1 - zh, x_=m4(x + d)) for d in (1, 2, 3)]
    for target in peers:
        pl.semaphore_signal(barrier, inc=1, device_id=target, device_id_type=MESH)

    for h in range(2):
        piece(G, zl, h, c, y)[...] = normalize(cells[h * 16:(h + 1) * 16, :], gain1[...])

    pl.semaphore_wait(barrier, len(peers))

    low, high = pl.ds(0, D // 2), pl.ds(D // 2, D // 2)

    def gather(middle):
        sends = []

        def send(ref, slot, target):
            cp = rcopy(ref, ref, slot, target)
            cp.start()
            sends.append(cp)
            return cp

        def mine(h):
            return piece(G, zl, h, c, y)

        zs, ys, near, far = {}, {}, [], []

        def hop(h, d):
            ys[h, d] = send(mine(h), AG_Y + h * 2 + d // 2, ydev[d])

        def arrive(h, d):
            ys[h, d].wait_recv()
            src = piece(G, zl, h, c, m4(y - d))
            zs[h, d] = send(src, AG_Z + h * 5 + d // 2 + 1, zdev[h])
            near.append(send(src, AG_NEAR + h * 4 + d // 2, sib))

        hop(0, 1)
        hop(1, 3)
        for h in range(2):
            zs[h, 0] = send(mine(h), AG_Z + h * 5, zdev[h])
            near.append(send(mine(h), AG_OWN + h, sib))
        arrive(0, 1)
        hop(1, 1)
        arrive(1, 3)
        hop(0, 3)
        fwd = {}

        def forward(h, d):
            lanes = low if d == 1 else high
            fwd[h, d] = send(piece(G, zl, h, c, m4(y - d)).at[:, lanes], AG_FWD + h * 2 + d // 2, ydev[d])

        arrive(1, 1)
        forward(0, 1)
        forward(1, 1)
        arrive(0, 3)
        forward(1, 3)
        forward(0, 3)
        for d in (1, 3):
            for h in range(2):
                fwd[h, d].wait_recv()
                src = piece(G, zl, h, c, m4(y + 2)).at[:, low if d == 1 else high]
                zs[h, d + 3] = send(src, AG_Z + h * 5 + 3 + d // 2, zdev[h])
                near.append(send(src, AG_NEAR + h * 4 + 2 + d // 2, sib))
        for cp in near:
            cp.wait_recv()
        middle()
        for i, d in enumerate((0, 1, 3, 4, 6)):
            for h in range(2):
                zs[h, d].wait_recv()
                src = piece(G, 1 - zl, h, c, m4(y - d if d < 4 else y + 2))
                if d > 3:
                    src = src.at[:, low if d == 4 else high]
                far.append(send(src, AG_FAR + h * 5 + i, sib))
        for cp in far:
            cp.wait_recv()
        for cp in sends:
            cp.wait_send()

    def scatter(produce, finish):
        sends = []

        def send(src, dst, slot, target):
            cp = rcopy(src, dst, slot, target)
            cp.start()
            sends.append(cp)
            return cp

        def add(slot, *others):
            total = slot[...].astype(F32)
            for other in others:
                total = total + other[...].astype(F32)
            slot[...] = total.astype(BF16)

        order = [(h, d) for d in (2, 1, 3, 0) for h in range(2)]
        cs, zs, ys, fwd = {}, {}, {}, {}

        def share(zrel):
            side = zl if zrel == 0 else 1 - zl
            for h, d in order:
                cs[h, d] = send(piece(PT, side, h, 1 - c, m4(y + d)), RC.at[zrel, h, d],
                                RS_C + zrel * 8 + h * 4 + d, sib)

        def pair_up(zrel, h, d):
            cs[h, d].wait_recv()
            add(RC.at[zrel, h, d], piece(PT, zl if zrel == 0 else 1 - zl, h, c, m4(y + d)))

        def cross(h, d):
            zs[h, d] = send(RC.at[1, h, d], RZ.at[h, d], RS_Z + h * 4 + d, zdev[h])

        produce(1 - zl)
        share(1)
        for h in range(2):
            pair_up(1, h, 2)
            cross(h, 2)
        for h, d in order[2:]:
            pair_up(1, h, d)
        cross(0, 1)
        cross(1, 3)
        produce(zl)
        share(0)
        for h in range(2):
            zs[h, 2].wait_send()
            cross(h, 3 if h == 0 else 1)
        for h in range(2):
            pair_up(0, h, 2)
            zs[h, 2].wait_recv()
            add(RC.at[0, h, 2], RZ.at[h, 2])
            for d, lanes in ((1, low), (3, high)):
                fwd[h, d] = send(RC.at[0, h, 2, :, lanes], RF.at[h, d // 2], RS_FWD + h * 2 + d // 2, ydev[d])
        for h, d in order[2:]:
            pair_up(0, h, d)
        for h in range(2):
            zs[h, 1 if h == 0 else 3].wait_send()
            cross(h, 0)
        for h, d in ((0, 1), (1, 3), (0, 3), (1, 1)):
            fwd[h, d].wait_recv()
            zs[h, d].wait_recv()
            first, second = (low, high) if d == 1 else (high, low)
            slot = RC.at[0, h, d]
            add(slot.at[:, first], RZ.at[h, d, :, first], RF.at[h, d // 2])
            add(slot.at[:, second], RZ.at[h, d, :, second])
            ys[h, d] = send(slot, RY.at[h, d // 2], RS_Y + h * 2 + d // 2, ydev[d])
        for h in range(2):
            zs[h, 0].wait_recv()
            sums = RC[0, h, 0].astype(F32) + RZ[h, 0].astype(F32)
            for d in (1, 3):
                ys[h, d].wait_recv()
                sums = sums + RY[h, d // 2].astype(F32)
            finish(h, sums)
        for cp in sends:
            if not any(cp is done for done in (zs[0, 2], zs[1, 2], zs[0, 1], zs[1, 3])):
                cp.wait_send()

    own_bias.start()
    bias_copies = {d: rcopy(bias_hbm.at[role(m4(x + d))[0]], BV.at[x], S_BIAS + d - 1, xdev[d]) for d in (1, 2, 3)}
    bias_copies[1].start()
    bias_copies[3].start()

    xc, own_x = {}, {}

    def place(zh_, zl_, pair_, part):
        return zh_ + pair_ * lax.rem(zl_ + part, 2) * (1 - 2 * zh_)

    def project(side, rel):
        lhs = G[rows(side * 256, 256), :]
        for j in range(3):
            acc = jnp.dot(lhs, wq[j], preferred_element_type=F32).reshape(2, 2, 4, 2, 8, 256)
            for h in range(2):
                for col in range(2):
                    tiles = [acc[h, cc, yy, col] for yy in range(4) for cc in range(2)]
                    val = jnp.concatenate(tiles, axis=0).astype(BF16)
                    for hd in range(2):
                        QB[hd, h * 2 + col, rows(side * 64, 64), j * 128:(j + 1) * 128] = val[:, hd * 128:(hd + 1) * 128]
        part = rows(side * 64, 64)
        for d in (2, 1, 3, 0):
            head_, pair_ = role(m4(x + d))
            src = QB.at[head_, pl.ds(pair_ * 2, 2), part]
            dst = XR.at[place(zh, zl, pair_, side), x, :, part]
            if d:
                xc[rel, d] = rcopy(src, dst, S_X + rel * 3 + d - 1, xdev[d])
                xc[rel, d].start()
            else:
                own_x[rel] = pltpu.make_async_copy(src, dst, lsem.at[1 + rel])
                own_x[rel].start()

    def first_project():
        wait(fetch_q)
        project(zl, 0)
        start(fetch_o)
        start(fetch_g)
        start(fetch_d)

    gather(first_project)
    project(1 - zl, 1)
    bias_copies[2].start()

    zc, zq = {}, {}
    for rel in range(2):
        side = zl if rel == 0 else 1 - zl
        part = rows(side * 64, 64)
        for d in (0, 1, 3, 2):
            if d:
                xc[rel, d].wait_recv()
            else:
                own_x[rel].wait()
            spot = (place(zh, zl, pair, side), m4(x - d), slice(None), part)
            if rel:
                ref = XR.at[spot + (pl.ds(0, 128),)]
                zq[d] = rcopy(ref, ref, S_ZQ + d, zhpart)
                pl.when(pair == 1)(zq[d].start)
            ref = XR.at[spot + (pl.ds(128, 256),)]
            zc[rel, d] = rcopy(ref, ref, S_ZH + rel * 4 + d, zhpart)
            zc[rel, d].start()
    wg[:, UNITS:UPAD, :] = jnp.zeros((2, UPAD - UNITS, D), BF16)
    wd[UNITS:UPAD, :] = jnp.zeros((UPAD - UNITS, D), BF16)
    own_bias.wait()
    for d in (1, 3, 2):
        bias_copies[d].wait_recv()
    for cp in zc.values():
        cp.wait_recv()
    for cp in zq.values():
        pl.when(pair == 1)(cp.wait_recv)

    ctx = {}
    local = {}
    for d in (2, 1, 3, 0):
        block = m4(x + d)
        heads_out = []
        for col in range(2):
            q = XR[zh, block, col, :, 0:128]
            k1 = XR[0, :, col, :, 128:256].reshape(512, 128)
            k2 = XR[1, :, col, :, 128:256].reshape(512, 128)
            dims = (((1,), (1,)), ((), ()))
            s1 = lax.dot_general(q, k1, dims, preferred_element_type=F32) * SCALE + BV[block, :, 0:512]
            s2 = lax.dot_general(q, k2, dims, preferred_element_type=F32) * SCALE + BV[block, :, 512:1024]
            peak = jnp.maximum(jnp.max(s1, axis=-1, keepdims=True), jnp.max(s2, axis=-1, keepdims=True))
            e1, e2 = jnp.exp(s1 - peak), jnp.exp(s2 - peak)
            total = jnp.sum(e1, axis=-1, keepdims=True) + jnp.sum(e2, axis=-1, keepdims=True)
            v1 = XR[0, :, col, :, 256:384].reshape(512, 128)
            v2 = XR[1, :, col, :, 256:384].reshape(512, 128)
            out = jnp.dot(e1.astype(BF16), v1, preferred_element_type=F32)
            out = out + jnp.dot(e2.astype(BF16), v2, preferred_element_type=F32)
            heads_out.append((out / total).reshape(2, 4, 2, 8, 128))
        tiles = [heads_out[col][zz, yy, cc] for zz in range(2) for cc in range(2) for yy in range(4) for col in range(2)]
        CS[block] = jnp.concatenate(tiles, axis=0).astype(BF16).reshape(2, 8, 16, 128)
        for rel in range(2):
            side = zl if rel == 0 else 1 - zl
            src, dst = CS.at[block, side], CH.at[head, side, pair]
            target = dev(zh_=place(zh, zl, pair, side), x_=block)
            slot = S_CTX + rel * 4 + d
            if d:
                ctx[rel, d] = rcopy(src, dst, slot, target)
                ctx[rel, d].start()
            else:
                local[rel] = pltpu.make_async_copy(src, dst, lsem.at[3 + rel])
                if rel == 0:
                    local[0].start()
                else:
                    ctx[1, 0] = rcopy(src, dst, slot, zhpart)
                    pl.when(pair == 1)(ctx[1, 0].start)
                    pl.when(pair == 0)(local[1].start)
    wait(fetch_o)
    for d in (2, 1, 3):
        for rel in range(2):
            ctx[rel, d].wait_recv()
    local[0].wait()
    pl.when(pair == 1)(ctx[1, 0].wait_recv)
    pl.when(pair == 0)(local[1].wait)

    def out_projection(side):
        @pl.loop(0, 8)
        def _(n):
            lhs = jnp.concatenate([CH[hd, side].reshape(256, 128) for hd in range(2)], axis=1)
            span = pl.ds(pl.multiple_of(n * 512, 512), 512)
            PT[rows(side * 256, 256), span] = jnp.dot(lhs, wo[:, span], preferred_element_type=F32).astype(BF16)

    def add_attended(h, sums):
        part = slice(h * 16, (h + 1) * 16)
        state[part, :] = (cells[part, :].astype(F32) + sums).astype(BF16)
        piece(G, zl, h, c, y)[...] = normalize(state[part, :], gain2[...])

    scatter(out_projection, add_attended)

    def units(side):
        @pl.loop(0, 3)
        def _(n):
            lhs = G[rows(side * 256, 256), :]
            span = rows(n * 256, 256)
            dims = (((1,), (1,)), ((), ()))
            gate = lax.dot_general(lhs, wg[0, span, :], dims, preferred_element_type=F32)
            up = lax.dot_general(lhs, wg[1, span, :], dims, preferred_element_type=F32)
            ACT[rows(side * 256, 256), pl.ds(pl.multiple_of(n * 256, 256), 256)] = (
                gate / (1.0 + jnp.exp(-gate)) * up).astype(BF16)

    def first_units():
        wait(fetch_g)
        units(zl)

    gather(first_units)
    units(1 - zl)
    wait(fetch_d)

    def down_projection(side):
        @pl.loop(0, 8)
        def _(n):
            span = pl.ds(pl.multiple_of(n * 512, 512), 512)
            PT[rows(side * 256, 256), span] = jnp.dot(
                ACT[rows(side * 256, 256), :], wd[:, span], preferred_element_type=F32).astype(BF16)

    def add_feed(h, sums):
        part = slice(h * 16, (h + 1) * 16)
        result[part, :] = (state[part, :].astype(F32) + sums).astype(BF16)

    scatter(down_projection, add_feed)
    for cp in [*bias_copies.values(), *xc.values(), *zc.values()]:
        cp.wait_send()
    for key, cp in ctx.items():
        if key != (1, 0):
            cp.wait_send()

    @pl.when(pair == 1)
    def _():
        for cp in [*zq.values(), ctx[1, 0]]:
            cp.wait_send()


def shards(cells, norm1_gain, w_qkv, row_bias, w_out, norm2_gain, w_gate_up, w_down):
    own = cells.transpose(1, 0, 2).reshape(32, D)
    vmem = pl.BlockSpec(memory_space=pltpu.VMEM)
    hbm = pl.BlockSpec(memory_space=pl.ANY)
    out = jax.ShapeDtypeStruct((32, D), BF16)
    state, result = pl.pallas_call(
        layer,
        out_shape=(out, out),
        in_specs=[vmem, vmem, hbm, hbm, hbm, vmem, hbm, hbm],
        out_specs=(vmem, vmem),
        scratch_shapes=[
            pltpu.VMEM((3, D, 256), BF16),
            pltpu.VMEM((256, D), BF16),
            pltpu.VMEM((2, UPAD, D), BF16),
            pltpu.VMEM((UPAD, D), BF16),
            pltpu.VMEM((512, D), BF16),
            pltpu.VMEM((512, D), BF16),
            pltpu.VMEM((2, 2, 4, 16, D), BF16),
            pltpu.VMEM((2, 4, 16, D), BF16),
            pltpu.VMEM((2, 2, 16, D), BF16),
            pltpu.VMEM((2, 2, 16, D // 2), BF16),
            pltpu.VMEM((4, 128, 1024), F32),
            pltpu.VMEM((2, 4, 128, 384), BF16),
            pltpu.VMEM((2, 4, 2, 128, 384), BF16),
            pltpu.VMEM((4, 2, 8, 16, 128), BF16),
            pltpu.VMEM((2, 2, 2, 8, 16, 128), BF16),
            pltpu.VMEM((512, UPAD), BF16),
            pltpu.SemaphoreType.DMA((N_SEM,)),
            pltpu.SemaphoreType.DMA((N_SEM,)),
            pltpu.SemaphoreType.DMA((36,)),
        ],
        compiler_params=pltpu.CompilerParams(
            collective_id=0, has_side_effects=True, vmem_limit_bytes=60 * 2**20),
        name="layer",
    )(own, norm1_gain.reshape(1, D), w_qkv.transpose(1, 0, 2), row_bias, w_out,
      norm2_gain.reshape(1, D), w_gate_up.transpose(1, 2, 0), w_down)
    return tuple(v.reshape(4, 8, D).transpose(1, 0, 2) for v in (state, result))


def solution(mesh):
    in_specs = (
        P(("row", "tensor"), None, None),
        P(),
        P(None, None, "tensor"),
        P("tensor", "row", None),
        P("tensor", None),
        P(),
        P(None, None, "tensor"),
        P("tensor", None),
    )
    out_specs = (P(("row", "tensor"), None, None), P(("row", "tensor"), None, None))
    return jax.shard_map(shards, mesh=mesh, in_specs=in_specs, out_specs=out_specs, check_vma=False)
```

```python
import functools
import math

import jax
import jax.numpy as jnp
from jax import lax
from jax.experimental import pallas as pl
from jax.experimental.pallas import tpu as pltpu
from jax.sharding import PartitionSpec as P

MESH = pl.DeviceIdType.MESH
F32 = jnp.float32
BF16 = jnp.bfloat16
D = 4096
UNITS = 688
UPAD = 768
SCALE = 1.0 / math.sqrt(128)

S_BIAS, S_X, S_ZH, S_ZQ, S_CTX = 0, 3, 9, 17, 21
AG_Z, AG_Y, AG_FWD, AG_OWN, AG_NEAR, AG_FAR = 29, 43, 51, 55, 57, 69
RS_C, RS_Z, RS_Y, RS_FWD = 83, 99, 115, 123
N_SEM = 127


def rows(start, count):
    return pl.ds(pl.multiple_of(start, 16), count)


def normalize(values, gain):
    wide = values.astype(F32)
    inverse = lax.rsqrt(jnp.mean(wide * wide, axis=-1, keepdims=True) + 1e-05)
    return (wide * inverse * gain).astype(BF16)


def layer(cells, gain1, wqkv_hbm, bias_hbm, wout_hbm, gain2, wgu_hbm, wdown_hbm, state, result,
          wq, wo, wg, wd, G, PT, RC, RZ, RY, RF, BV, QB, XR, CS, CH, ACT, ssem, rsem, lsem):
    r = lax.axis_index("row")
    t = lax.axis_index("tensor")
    zh, x = r // 4, lax.rem(r, 4)
    k, c = t // 2, lax.rem(t, 2)
    zl, y = k // 4, lax.rem(k, 4)

    def m4(v):
        return lax.rem(v + 4, 4)

    def role(x_):
        turn = m4(x_ + c)
        return turn // 2, lax.rem(turn, 2)

    head, pair = role(x)

    def dev(zh_=zh, x_=x, zl_=zl, y_=y, c_=c):
        return (zh_ * 4 + x_, zl_ * 8 + y_ * 2 + c_)

    sib = dev(c_=1 - c)
    zdev = (dev(zl_=1 - zl), dev(zh_=1 - zh, zl_=1 - zl))
    ydev = {d: dev(y_=m4(y + d)) for d in (1, 2, 3)}
    xdev = {d: dev(x_=m4(x + d)) for d in (1, 2, 3)}
    zhpart = dev(zh_=1 - zh)

    def piece(ref, zl_, h, c_, y_):
        return ref.at[rows((zl_ * 16 + h * 8 + c_ * 4 + y_) * 16, 16)]

    def rcopy(src, dst, slot, target):
        return pltpu.make_async_remote_copy(
            src_ref=src, dst_ref=dst, send_sem=ssem.at[slot], recv_sem=rsem.at[slot],
            device_id=target, device_id_type=MESH)

    def fetch(pairs, slot):
        return [pltpu.make_async_copy(src, dst, lsem.at[slot + i]) for i, (src, dst) in enumerate(pairs)]

    own_bias = pltpu.make_async_copy(bias_hbm.at[head], BV.at[x], lsem.at[0])
    fetch_q = fetch([(wqkv_hbm.at[j, pl.ds(i * 1024, 1024)], wq.at[j, pl.ds(i * 1024, 1024)])
                     for j in range(3) for i in range(4)], 8)
    fetch_o = fetch([(wout_hbm.at[pl.ds(i * 64, 64)], wo.at[pl.ds(i * 64, 64)]) for i in range(4)], 20)
    fetch_g = fetch([(wgu_hbm.at[j, pl.ds(i * 176, w)], wg.at[j, pl.ds(i * 176, w)])
                     for i, w in enumerate((176, 176, 176, 160)) for j in range(2)], 24)
    fetch_d = fetch([(wdown_hbm.at[pl.ds(i * 176, w)], wd.at[pl.ds(i * 176, w)])
                     for i, w in enumerate((176, 176, 176, 160))], 32)

    def start(copies):
        for cp in copies:
            cp.start()

    def wait(copies):
        for cp in copies:
            cp.wait()

    start(fetch_q)

    barrier = pltpu.get_barrier_semaphore()
    peers = [sib, zdev[0], zdev[1], zhpart] + [ydev[d] for d in (1, 2, 3)] + [xdev[d] for d in (1, 2, 3)]
    peers += [dev(zh_=1 - zh, x_=m4(x + d)) for d in (1, 2, 3)]
    for target in peers:
        pl.semaphore_signal(barrier, inc=1, device_id=target, device_id_type=MESH)

    for h in range(2):
        piece(G, zl, h, c, y)[...] = normalize(cells[h * 16:(h + 1) * 16, :], gain1[...])

    pl.semaphore_wait(barrier, len(peers))

    lanes = (pl.ds(0, D // 2), pl.ds(D // 2, D // 2))
    turns = ((0, 1), (1, 3), (1, 1), (0, 3))

    def first(d):
        return d // 2

    def gather(middle):
        sends = []

        def send(ref, slot, target):
            cp = rcopy(ref, ref, slot, target)
            cp.start()
            sends.append(cp)
            return cp

        zs, ys, fwd, near, far = {}, {}, {}, [], []
        steps = [(h, d, first(d)) for h, d in turns] + [(h, d, 1 - first(d)) for h, d in turns]
        ahead = [(h, 2, first(d)) for h, d in turns]

        def own(h):
            return piece(G, zl, h, c, y)

        def hop(h, d, i):
            ys[h, d, i] = send(own(h).at[:, lanes[i]], AG_Y + h * 4 + first(d) * 2 + i, ydev[d])

        def spot(zl_, h, d, i):
            return piece(G, zl_, h, c, m4(y - d)).at[:, lanes[i]]

        def spread(h, d, i):
            src = spot(zl, h, d, i)
            zs[h, d, i] = send(src, AG_Z + h * 7 + d * 2 + i - 1, zdev[h])
            near.append(send(src, AG_NEAR + h * 6 + d * 2 + i - 2, sib))

        def arrive(h, d, i):
            ys[h, d, i].wait_recv()
            if i == first(d):
                fwd[h, i] = send(spot(zl, h, d, i), AG_FWD + h * 2 + i, ydev[d])
            spread(h, d, i)

        def cross(h, d, i):
            zs[h, d, i].wait_recv()
            far.append(send(spot(1 - zl, h, d, i), AG_FAR + h * 7 + d * 2 + i - 1, sib))

        for step in steps[:4]:
            hop(*step)
        for h in range(2):
            zs[h, 0] = send(own(h), AG_Z + h * 7, zdev[h])
        for step in steps[4:]:
            hop(*step)
        for h in range(2):
            near.append(send(own(h), AG_OWN + h, sib))
        for step in steps[:4]:
            arrive(*step)
        for h in range(2):
            zs[h, 0].wait_recv()
            far.append(send(piece(G, 1 - zl, h, c, y), AG_FAR + h * 7, sib))
        for step in steps[4:]:
            arrive(*step)
        for step in steps[:4]:
            cross(*step)
        for h, d, i in ahead:
            fwd[h, i].wait_recv()
            spread(h, d, i)
        for cp in near:
            cp.wait_recv()
        middle()
        for step in steps[4:] + ahead:
            cross(*step)
        for cp in far:
            cp.wait_recv()
        for cp in sends:
            cp.wait_send()

    def scatter(produce, finish):
        sends = []

        def send(src, dst, slot, target):
            cp = rcopy(src, dst, slot, target)
            cp.start()
            sends.append(cp)
            return cp

        def add(slot, *others):
            total = slot[...].astype(F32)
            for other in others:
                total = total + other[...].astype(F32)
            slot[...] = total.astype(BF16)

        order = [(0, 2), (1, 2), *turns, (0, 0), (1, 0)]
        cs, zs, ys, fwd = {}, {}, {}, {}

        def share(zrel):
            side = zl if zrel == 0 else 1 - zl
            for h, d in order:
                cs[h, d] = send(piece(PT, side, h, 1 - c, m4(y + d)), RC.at[zrel, h, d],
                                RS_C + zrel * 8 + h * 4 + d, sib)

        def pair_up(zrel, h, d):
            cs[h, d].wait_recv()
            add(RC.at[zrel, h, d], piece(PT, zl if zrel == 0 else 1 - zl, h, c, m4(y + d)))

        def cross(h, d, i):
            zs[h, d, i] = send(RC.at[1, h, d, :, lanes[i]], RZ.at[h, d, :, lanes[i]],
                               RS_Z + h * 8 + d * 2 + i, zdev[h])

        def hop(h, d, i, *others):
            zs[h, d, i].wait_recv()
            slot = RC.at[0, h, d, :, lanes[i]]
            add(slot, RZ.at[h, d, :, lanes[i]], *others)
            ys[h, d, i] = send(slot, RY.at[h, first(d), :, lanes[i]], RS_Y + h * 4 + first(d) * 2 + i, ydev[d])

        produce(1 - zl)
        share(1)
        for h in range(2):
            pair_up(1, h, 2)
            for i in range(2):
                cross(h, 2, i)
        for h, d in turns:
            pair_up(1, h, d)
            cross(h, d, 1 - first(d))
        for h, d in turns:
            cross(h, d, first(d))
        for h in range(2):
            pair_up(1, h, 0)
            for i in range(2):
                cross(h, 0, i)
        produce(zl)
        share(0)
        for h in range(2):
            pair_up(0, h, 2)
            for i, d in ((0, 1), (1, 3)):
                zs[h, 2, i].wait_recv()
                slot = RC.at[0, h, 2, :, lanes[i]]
                add(slot, RZ.at[h, 2, :, lanes[i]])
                fwd[h, i] = send(slot, RF.at[h, i], RS_FWD + h * 2 + i, ydev[d])
        for h, d in turns:
            pair_up(0, h, d)
            hop(h, d, 1 - first(d))
        for h, d in turns:
            fwd[h, first(d)].wait_recv()
            hop(h, d, first(d), RF.at[h, first(d)])
        for h in range(2):
            pair_up(0, h, 0)
        for h in range(2):
            for i in range(2):
                zs[h, 0, i].wait_recv()
            sums = RC[0, h, 0].astype(F32) + RZ[h, 0].astype(F32)
            for d in (1, 3):
                for i in range(2):
                    ys[h, d, i].wait_recv()
                sums = sums + RY[h, first(d)].astype(F32)
            finish(h, sums)
        for cp in sends:
            cp.wait_send()

    own_bias.start()
    bias_copies = {d: rcopy(bias_hbm.at[role(m4(x + d))[0]], BV.at[x], S_BIAS + d - 1, xdev[d]) for d in (1, 2, 3)}
    bias_copies[1].start()
    bias_copies[3].start()

    xc, own_x = {}, {}

    def place(zh_, zl_, pair_, part):
        return zh_ + pair_ * lax.rem(zl_ + part, 2) * (1 - 2 * zh_)

    def project(side, rel):
        lhs = G[rows(side * 256, 256), :]
        for j in range(3):
            acc = jnp.dot(lhs, wq[j], preferred_element_type=F32).reshape(2, 2, 4, 2, 8, 256)
            for h in range(2):
                for col in range(2):
                    tiles = [acc[h, cc, yy, col] for yy in range(4) for cc in range(2)]
                    val = jnp.concatenate(tiles, axis=0).astype(BF16)
                    for hd in range(2):
                        QB[hd, h * 2 + col, rows(side * 64, 64), j * 128:(j + 1) * 128] = val[:, hd * 128:(hd + 1) * 128]
        part = rows(side * 64, 64)
        for d in (2, 1, 3, 0):
            head_, pair_ = role(m4(x + d))
            src = QB.at[head_, pl.ds(pair_ * 2, 2), part]
            dst = XR.at[place(zh, zl, pair_, side), x, :, part]
            if d:
                xc[rel, d] = rcopy(src, dst, S_X + rel * 3 + d - 1, xdev[d])
                xc[rel, d].start()
            else:
                own_x[rel] = pltpu.make_async_copy(src, dst, lsem.at[1 + rel])
                own_x[rel].start()

    def first_project():
        wait(fetch_q)
        project(zl, 0)
        start(fetch_o)
        start(fetch_g)
        start(fetch_d)

    gather(first_project)
    project(1 - zl, 1)
    bias_copies[2].start()

    zc, zq = {}, {}
    for rel in range(2):
        side = zl if rel == 0 else 1 - zl
        part = rows(side * 64, 64)
        for d in (0, 1, 3, 2):
            if d:
                xc[rel, d].wait_recv()
            else:
                own_x[rel].wait()
            spot = (place(zh, zl, pair, side), m4(x - d), slice(None), part)
            if rel:
                ref = XR.at[spot + (pl.ds(0, 128),)]
                zq[d] = rcopy(ref, ref, S_ZQ + d, zhpart)
                pl.when(pair == 1)(zq[d].start)
            ref = XR.at[spot + (pl.ds(128, 256),)]
            zc[rel, d] = rcopy(ref, ref, S_ZH + rel * 4 + d, zhpart)
            zc[rel, d].start()
    wg[:, UNITS:UPAD, :] = jnp.zeros((2, UPAD - UNITS, D), BF16)
    wd[UNITS:UPAD, :] = jnp.zeros((UPAD - UNITS, D), BF16)
    own_bias.wait()
    for d in (1, 3, 2):
        bias_copies[d].wait_recv()
    for cp in zc.values():
        cp.wait_recv()
    for cp in zq.values():
        pl.when(pair == 1)(cp.wait_recv)

    ctx = {}
    local = {}
    for d in (2, 1, 3, 0):
        block = m4(x + d)
        heads_out = []
        for col in range(2):
            q = XR[zh, block, col, :, 0:128]
            k1 = XR[0, :, col, :, 128:256].reshape(512, 128)
            k2 = XR[1, :, col, :, 128:256].reshape(512, 128)
            dims = (((1,), (1,)), ((), ()))
            s1 = lax.dot_general(q, k1, dims, preferred_element_type=F32) * SCALE + BV[block, :, 0:512]
            s2 = lax.dot_general(q, k2, dims, preferred_element_type=F32) * SCALE + BV[block, :, 512:1024]
            peak = jnp.maximum(jnp.max(s1, axis=-1, keepdims=True), jnp.max(s2, axis=-1, keepdims=True))
            e1, e2 = jnp.exp(s1 - peak), jnp.exp(s2 - peak)
            total = jnp.sum(e1, axis=-1, keepdims=True) + jnp.sum(e2, axis=-1, keepdims=True)
            v1 = XR[0, :, col, :, 256:384].reshape(512, 128)
            v2 = XR[1, :, col, :, 256:384].reshape(512, 128)
            out = jnp.dot(e1.astype(BF16), v1, preferred_element_type=F32)
            out = out + jnp.dot(e2.astype(BF16), v2, preferred_element_type=F32)
            heads_out.append((out / total).reshape(2, 4, 2, 8, 128))
        tiles = [heads_out[col][zz, yy, cc] for zz in range(2) for cc in range(2) for yy in range(4) for col in range(2)]
        CS[block] = jnp.concatenate(tiles, axis=0).astype(BF16).reshape(2, 8, 16, 128)
        for rel in range(2):
            side = zl if rel == 0 else 1 - zl
            src, dst = CS.at[block, side], CH.at[head, side, pair]
            target = dev(zh_=place(zh, zl, pair, side), x_=block)
            slot = S_CTX + rel * 4 + d
            if d:
                ctx[rel, d] = rcopy(src, dst, slot, target)
                ctx[rel, d].start()
            else:
                local[rel] = pltpu.make_async_copy(src, dst, lsem.at[3 + rel])
                if rel == 0:
                    local[0].start()
                else:
                    ctx[1, 0] = rcopy(src, dst, slot, zhpart)
                    pl.when(pair == 1)(ctx[1, 0].start)
                    pl.when(pair == 0)(local[1].start)
    wait(fetch_o)
    for d in (2, 1, 3):
        for rel in range(2):
            ctx[rel, d].wait_recv()
    local[0].wait()
    pl.when(pair == 1)(ctx[1, 0].wait_recv)
    pl.when(pair == 0)(local[1].wait)

    def out_projection(side):
        @pl.loop(0, 8)
        def _(n):
            lhs = jnp.concatenate([CH[hd, side].reshape(256, 128) for hd in range(2)], axis=1)
            span = pl.ds(pl.multiple_of(n * 512, 512), 512)
            PT[rows(side * 256, 256), span] = jnp.dot(lhs, wo[:, span], preferred_element_type=F32).astype(BF16)

    def add_attended(h, sums):
        part = slice(h * 16, (h + 1) * 16)
        state[part, :] = (cells[part, :].astype(F32) + sums).astype(BF16)
        piece(G, zl, h, c, y)[...] = normalize(state[part, :], gain2[...])

    scatter(out_projection, add_attended)

    def units(side):
        @pl.loop(0, 3)
        def _(n):
            lhs = G[rows(side * 256, 256), :]
            span = rows(n * 256, 256)
            dims = (((1,), (1,)), ((), ()))
            gate = lax.dot_general(lhs, wg[0, span, :], dims, preferred_element_type=F32)
            up = lax.dot_general(lhs, wg[1, span, :], dims, preferred_element_type=F32)
            ACT[rows(side * 256, 256), pl.ds(pl.multiple_of(n * 256, 256), 256)] = (
                gate / (1.0 + jnp.exp(-gate)) * up).astype(BF16)

    def first_units():
        wait(fetch_g)
        units(zl)

    gather(first_units)
    units(1 - zl)
    wait(fetch_d)

    def down_projection(side):
        @pl.loop(0, 8)
        def _(n):
            span = pl.ds(pl.multiple_of(n * 512, 512), 512)
            PT[rows(side * 256, 256), span] = jnp.dot(
                ACT[rows(side * 256, 256), :], wd[:, span], preferred_element_type=F32).astype(BF16)

    def add_feed(h, sums):
        part = slice(h * 16, (h + 1) * 16)
        result[part, :] = (state[part, :].astype(F32) + sums).astype(BF16)

    scatter(down_projection, add_feed)
    for cp in [*bias_copies.values(), *xc.values(), *zc.values()]:
        cp.wait_send()
    for key, cp in ctx.items():
        if key != (1, 0):
            cp.wait_send()

    @pl.when(pair == 1)
    def _():
        for cp in [*zq.values(), ctx[1, 0]]:
            cp.wait_send()


def shards(cells, norm1_gain, w_qkv, row_bias, w_out, norm2_gain, w_gate_up, w_down):
    own = cells.transpose(1, 0, 2).reshape(32, D)
    vmem = pl.BlockSpec(memory_space=pltpu.VMEM)
    hbm = pl.BlockSpec(memory_space=pl.ANY)
    out = jax.ShapeDtypeStruct((32, D), BF16)
    state, result = pl.pallas_call(
        layer,
        out_shape=(out, out),
        in_specs=[vmem, vmem, hbm, hbm, hbm, vmem, hbm, hbm],
        out_specs=(vmem, vmem),
        scratch_shapes=[
            pltpu.VMEM((3, D, 256), BF16),
            pltpu.VMEM((256, D), BF16),
            pltpu.VMEM((2, UPAD, D), BF16),
            pltpu.VMEM((UPAD, D), BF16),
            pltpu.VMEM((512, D), BF16),
            pltpu.VMEM((512, D), BF16),
            pltpu.VMEM((2, 2, 4, 16, D), BF16),
            pltpu.VMEM((2, 4, 16, D), BF16),
            pltpu.VMEM((2, 2, 16, D), BF16),
            pltpu.VMEM((2, 2, 16, D // 2), BF16),
            pltpu.VMEM((4, 128, 1024), F32),
            pltpu.VMEM((2, 4, 128, 384), BF16),
            pltpu.VMEM((2, 4, 2, 128, 384), BF16),
            pltpu.VMEM((4, 2, 8, 16, 128), BF16),
            pltpu.VMEM((2, 2, 2, 8, 16, 128), BF16),
            pltpu.VMEM((512, UPAD), BF16),
            pltpu.SemaphoreType.DMA((N_SEM,)),
            pltpu.SemaphoreType.DMA((N_SEM,)),
            pltpu.SemaphoreType.DMA((36,)),
        ],
        compiler_params=pltpu.CompilerParams(
            collective_id=0, has_side_effects=True, vmem_limit_bytes=60 * 2**20),
        name="layer",
    )(own, norm1_gain.reshape(1, D), w_qkv.transpose(1, 0, 2), row_bias, w_out,
      norm2_gain.reshape(1, D), w_gate_up.transpose(1, 2, 0), w_down)
    return tuple(v.reshape(4, 8, D).transpose(1, 0, 2) for v in (state, result))


def solution(mesh):
    in_specs = (
        P(("row", "tensor"), None, None),
        P(),
        P(None, None, "tensor"),
        P("tensor", "row", None),
        P("tensor", None),
        P(),
        P(None, None, "tensor"),
        P("tensor", None),
    )
    out_specs = (P(("row", "tensor"), None, None), P(("row", "tensor"), None, None))
    return jax.shard_map(shards, mesh=mesh, in_specs=in_specs, out_specs=out_specs, check_vma=False)
```

```python
import functools
import math

import jax
import jax.numpy as jnp
from jax import lax
from jax.experimental import pallas as pl
from jax.experimental.pallas import tpu as pltpu
from jax.sharding import PartitionSpec as P

MESH = pl.DeviceIdType.MESH
F32 = jnp.float32
BF16 = jnp.bfloat16
D = 4096
UNITS = 688
UPAD = 768
SCALE = 1.0 / math.sqrt(128)

S_BIAS, S_X, S_ZH, S_ZQ, S_CTX = 0, 3, 9, 17, 21
AG_Z, AG_Y, AG_FWD, AG_OWN, AG_NEAR, AG_FAR = 29, 43, 51, 55, 57, 69
RS_C, RS_Z, RS_Y, RS_FWD = 83, 115, 131, 139
N_SEM = 143


def rows(start, count):
    return pl.ds(pl.multiple_of(start, 16), count)


def normalize(values, gain):
    wide = values.astype(F32)
    inverse = lax.rsqrt(jnp.mean(wide * wide, axis=-1, keepdims=True) + 1e-05)
    return (wide * inverse * gain).astype(BF16)


def layer(cells, gain1, wqkv_hbm, bias_hbm, wout_hbm, gain2, wgu_hbm, wdown_hbm, state, result,
          wq, wo, wg, wd, mix, own, G, PT, RC, RZ, RY, RF, BV, QB, XR, CS, CH, ACT, ssem, rsem, lsem):
    r = lax.axis_index("row")
    t = lax.axis_index("tensor")
    zh, x = r // 4, lax.rem(r, 4)
    k, c = t // 2, lax.rem(t, 2)
    zl, y = k // 4, lax.rem(k, 4)

    def m4(v):
        return lax.rem(v + 4, 4)

    def role(x_):
        turn = m4(x_ + c)
        return turn // 2, lax.rem(turn, 2)

    head, pair = role(x)

    def dev(zh_=zh, x_=x, zl_=zl, y_=y, c_=c):
        return (zh_ * 4 + x_, zl_ * 8 + y_ * 2 + c_)

    sib = dev(c_=1 - c)
    zdev = (dev(zl_=1 - zl), dev(zh_=1 - zh, zl_=1 - zl))
    ydev = {d: dev(y_=m4(y + d)) for d in (1, 2, 3)}
    xdev = {d: dev(x_=m4(x + d)) for d in (1, 2, 3)}
    zhpart = dev(zh_=1 - zh)

    def piece(ref, zl_, h, c_, y_):
        return ref.at[rows((zl_ * 16 + h * 8 + c_ * 4 + y_) * 16, 16)]

    def rcopy(src, dst, slot, target):
        return pltpu.make_async_remote_copy(
            src_ref=src, dst_ref=dst, send_sem=ssem.at[slot], recv_sem=rsem.at[slot],
            device_id=target, device_id_type=MESH)

    def fetch(pairs, slot):
        return [pltpu.make_async_copy(src, dst, lsem.at[slot + i]) for i, (src, dst) in enumerate(pairs)]

    own_bias = pltpu.make_async_copy(bias_hbm.at[head], BV.at[x], lsem.at[0])
    fetch_q = fetch([(wqkv_hbm.at[j, pl.ds(i * 1024, 1024)], wq.at[j, pl.ds(i * 1024, 1024)])
                     for j in range(3) for i in range(4)], 8)
    fetch_o = fetch([(wout_hbm.at[pl.ds(i * 64, 64)], wo.at[pl.ds(i * 64, 64)]) for i in range(4)], 20)
    fetch_g = fetch([(wgu_hbm.at[j, pl.ds(i * 176, w)], wg.at[j, pl.ds(i * 176, w)])
                     for i, w in enumerate((176, 176, 176, 160)) for j in range(2)], 24)
    fetch_d = fetch([(wdown_hbm.at[pl.ds(i * 176, w)], wd.at[pl.ds(i * 176, w)])
                     for i, w in enumerate((176, 176, 176, 160))], 32)

    def start(copies):
        for cp in copies:
            cp.start()

    def wait(copies):
        for cp in copies:
            cp.wait()

    start(fetch_q)

    barrier = pltpu.get_barrier_semaphore()
    peers = [sib, zdev[0], zdev[1], zhpart] + [ydev[d] for d in (1, 2, 3)] + [xdev[d] for d in (1, 2, 3)]
    peers += [dev(zh_=1 - zh, x_=m4(x + d)) for d in (1, 2, 3)]
    for target in peers:
        pl.semaphore_signal(barrier, inc=1, device_id=target, device_id_type=MESH)

    @pl.loop(0, D // 128)
    def _(n):
        lane = pl.ds(pl.multiple_of(n * 128, 128), 128)
        for i in range(8):
            mix[i * 4:(i + 1) * 4, :] = cells[i, :, lane].astype(F32)
        for col in range(4):
            own[col * 8:(col + 1) * 8, lane] = mix[pl.ds(col, 8, stride=4), :]

    for h in range(2):
        piece(G, zl, h, c, y)[...] = normalize(own[h * 16:(h + 1) * 16, :], gain1[...])

    pl.semaphore_wait(barrier, len(peers))

    lanes = (pl.ds(0, D // 2), pl.ds(D // 2, D // 2))
    turns = ((0, 1), (1, 3), (1, 1), (0, 3))

    def first(d):
        return d // 2

    def gather(middle):
        sends = []

        def send(ref, slot, target):
            cp = rcopy(ref, ref, slot, target)
            cp.start()
            sends.append(cp)
            return cp

        zs, ys, fwd, near, far = {}, {}, {}, [], []
        steps = [(h, d, first(d)) for h, d in turns] + [(h, d, 1 - first(d)) for h, d in turns]
        ahead = [(h, 2, first(d)) for h, d in turns]

        def own(h):
            return piece(G, zl, h, c, y)

        def hop(h, d, i):
            ys[h, d, i] = send(own(h).at[:, lanes[i]], AG_Y + h * 4 + first(d) * 2 + i, ydev[d])

        def spot(zl_, h, d, i):
            return piece(G, zl_, h, c, m4(y - d)).at[:, lanes[i]]

        def spread(h, d, i):
            src = spot(zl, h, d, i)
            zs[h, d, i] = send(src, AG_Z + h * 7 + d * 2 + i - 1, zdev[h])
            near.append(send(src, AG_NEAR + h * 6 + d * 2 + i - 2, sib))

        def arrive(h, d, i):
            ys[h, d, i].wait_recv()
            if i == first(d):
                fwd[h, i] = send(spot(zl, h, d, i), AG_FWD + h * 2 + i, ydev[d])
            spread(h, d, i)

        def cross(h, d, i):
            zs[h, d, i].wait_recv()
            far.append(send(spot(1 - zl, h, d, i), AG_FAR + h * 7 + d * 2 + i - 1, sib))

        for step in steps[:4]:
            hop(*step)
        for h in range(2):
            zs[h, 0] = send(own(h), AG_Z + h * 7, zdev[h])
        for step in steps[4:]:
            hop(*step)
        for h in range(2):
            near.append(send(own(h), AG_OWN + h, sib))
        for step in steps[:4]:
            arrive(*step)
        for h in range(2):
            zs[h, 0].wait_recv()
            far.append(send(piece(G, 1 - zl, h, c, y), AG_FAR + h * 7, sib))
        for step in steps[4:]:
            arrive(*step)
        for step in steps[:4]:
            cross(*step)
        for h, d, i in ahead:
            fwd[h, i].wait_recv()
            spread(h, d, i)
        for cp in near:
            cp.wait_recv()
        middle[0]()
        for step in steps[4:]:
            cross(*step)
        middle[1]()
        for step in ahead:
            cross(*step)
        middle[2]()
        for cp in far:
            cp.wait_recv()
        for cp in sends:
            cp.wait_send()

    def scatter(produce, finish):
        sends = []

        def send(src, dst, slot, target):
            cp = rcopy(src, dst, slot, target)
            cp.start()
            sends.append(cp)
            return cp

        def add(slot, *others):
            total = slot[...].astype(F32)
            for other in others:
                total = total + other[...].astype(F32)
            slot[...] = total.astype(BF16)

        order = [(0, 2), (1, 2), *turns, (0, 0), (1, 0)]
        cs, zs, ys, fwd = {}, {}, {}, {}

        def share(zrel):
            side = zl if zrel == 0 else 1 - zl
            for i in range(2):
                produce(side, i)
                for h, d in order:
                    cs[h, d, i] = send(piece(PT, side, h, 1 - c, m4(y + d)).at[:, lanes[i]],
                                       RC.at[zrel, h, d, :, lanes[i]], RS_C + zrel * 16 + h * 8 + d * 2 + i, sib)

        def pair_up(zrel, h, d, i):
            cs[h, d, i].wait_recv()
            side = zl if zrel == 0 else 1 - zl
            add(RC.at[zrel, h, d, :, lanes[i]], piece(PT, side, h, c, m4(y + d)).at[:, lanes[i]])

        def cross(h, d, i):
            pair_up(1, h, d, i)
            zs[h, d, i] = send(RC.at[1, h, d, :, lanes[i]], RZ.at[h, d, :, lanes[i]],
                               RS_Z + h * 8 + d * 2 + i, zdev[h])

        def hop(h, d, i, *others):
            pair_up(0, h, d, i)
            zs[h, d, i].wait_recv()
            slot = RC.at[0, h, d, :, lanes[i]]
            add(slot, RZ.at[h, d, :, lanes[i]], *others)
            ys[h, d, i] = send(slot, RY.at[h, first(d), :, lanes[i]], RS_Y + h * 4 + first(d) * 2 + i, ydev[d])

        share(1)
        for i, d in ((0, 3), (1, 1)):
            for h in range(2):
                cross(h, 2, i)
            for h in range(2):
                cross(h, d, i)
        for h, d in turns:
            cross(h, d, first(d))
        for h in range(2):
            for i in range(2):
                cross(h, 0, i)
        share(0)
        for i, d in ((0, 1), (1, 3)):
            for h in range(2):
                pair_up(0, h, 2, i)
                zs[h, 2, i].wait_recv()
                slot = RC.at[0, h, 2, :, lanes[i]]
                add(slot, RZ.at[h, 2, :, lanes[i]])
                fwd[h, i] = send(slot, RF.at[h, i], RS_FWD + h * 2 + i, ydev[d])
        for h, d in turns:
            hop(h, d, 1 - first(d))
        for h, d in turns:
            fwd[h, first(d)].wait_recv()
            hop(h, d, first(d), RF.at[h, first(d)])
        for h in range(2):
            for i in range(2):
                pair_up(0, h, 0, i)
        for h in range(2):
            for i in range(2):
                zs[h, 0, i].wait_recv()
            sums = RC[0, h, 0].astype(F32) + RZ[h, 0].astype(F32)
            for d in (1, 3):
                for i in range(2):
                    ys[h, d, i].wait_recv()
                sums = sums + RY[h, first(d)].astype(F32)
            finish(h, sums)
        for cp in sends:
            cp.wait_send()

    own_bias.start()
    bias_copies = {d: rcopy(bias_hbm.at[role(m4(x + d))[0]], BV.at[x], S_BIAS + d - 1, xdev[d]) for d in (1, 2, 3)}
    for d in (1, 3):
        bias_copies[d].start()

    xc, own_x = {}, {}

    def place(zh_, zl_, pair_, part):
        return zh_ + pair_ * lax.rem(zl_ + part, 2) * (1 - 2 * zh_)

    def project(side, j):
        lhs = G[rows(side * 256, 256), :]
        acc = jnp.dot(lhs, wq[j], preferred_element_type=F32).reshape(2, 2, 4, 2, 8, 256)
        for h in range(2):
            for col in range(2):
                tiles = [acc[h, cc, yy, col] for yy in range(4) for cc in range(2)]
                val = jnp.concatenate(tiles, axis=0).astype(BF16)
                for hd in range(2):
                    QB[hd, h * 2 + col, rows(side * 64, 64), j * 128:(j + 1) * 128] = val[:, hd * 128:(hd + 1) * 128]

    def ship(side, rel):
        part = rows(side * 64, 64)
        for d in (2, 1, 3, 0):
            head_, pair_ = role(m4(x + d))
            src = QB.at[head_, pl.ds(pair_ * 2, 2), part]
            dst = XR.at[place(zh, zl, pair_, side), x, :, part]
            if d:
                xc[rel, d] = rcopy(src, dst, S_X + rel * 3 + d - 1, xdev[d])
                xc[rel, d].start()
            else:
                own_x[rel] = pltpu.make_async_copy(src, dst, lsem.at[1 + rel])
                own_x[rel].start()

    def last_step():
        project(zl, 2)
        ship(zl, 0)
        start(fetch_o)
        start(fetch_g)
        start(fetch_d)

    wait(fetch_q)
    gather([functools.partial(project, zl, 0), functools.partial(project, zl, 1), last_step])

    zc, zq = {}, {}

    def pass_on(side, rel):
        part = rows(side * 64, 64)
        for d in (0, 1, 3, 2):
            if d:
                xc[rel, d].wait_recv()
            else:
                own_x[rel].wait()
            spot = (place(zh, zl, pair, side), m4(x - d), slice(None), part)
            if rel:
                ref = XR.at[spot + (pl.ds(0, 128),)]
                zq[d] = rcopy(ref, ref, S_ZQ + d, zhpart)
                pl.when(pair == 1)(zq[d].start)
            ref = XR.at[spot + (pl.ds(128, 256),)]
            zc[rel, d] = rcopy(ref, ref, S_ZH + rel * 4 + d, zhpart)
            zc[rel, d].start()

    for j in range(3):
        project(1 - zl, j)
    ship(1 - zl, 1)
    bias_copies[2].start()
    pass_on(zl, 0)
    pass_on(1 - zl, 1)
    wg[:, UNITS:UPAD, :] = jnp.zeros((2, UPAD - UNITS, D), BF16)
    wd[UNITS:UPAD, :] = jnp.zeros((UPAD - UNITS, D), BF16)
    own_bias.wait()
    for d in (1, 3):
        bias_copies[d].wait_recv()
    for cp in zc.values():
        cp.wait_recv()
    for cp in zq.values():
        pl.when(pair == 1)(cp.wait_recv)

    ctx = {}
    local = {}
    for d in (1, 3, 0, 2):
        block = m4(x + d)
        heads_out = []
        if d == 2:
            bias_copies[2].wait_recv()
        for col in range(2):
            q = XR[zh, block, col, :, 0:128]
            k1 = XR[0, :, col, :, 128:256].reshape(512, 128)
            k2 = XR[1, :, col, :, 128:256].reshape(512, 128)
            dims = (((1,), (1,)), ((), ()))
            s1 = lax.dot_general(q, k1, dims, preferred_element_type=F32) * SCALE + BV[block, :, 0:512]
            s2 = lax.dot_general(q, k2, dims, preferred_element_type=F32) * SCALE + BV[block, :, 512:1024]
            peak = jnp.maximum(jnp.max(s1, axis=-1, keepdims=True), jnp.max(s2, axis=-1, keepdims=True))
            e1, e2 = jnp.exp(s1 - peak), jnp.exp(s2 - peak)
            total = jnp.sum(e1, axis=-1, keepdims=True) + jnp.sum(e2, axis=-1, keepdims=True)
            v1 = XR[0, :, col, :, 256:384].reshape(512, 128)
            v2 = XR[1, :, col, :, 256:384].reshape(512, 128)
            out = jnp.dot(e1.astype(BF16), v1, preferred_element_type=F32)
            out = out + jnp.dot(e2.astype(BF16), v2, preferred_element_type=F32)
            heads_out.append((out / total).reshape(2, 4, 2, 8, 128))
        tiles = [heads_out[col][zz, yy, cc] for zz in range(2) for cc in range(2) for yy in range(4) for col in range(2)]
        CS[block] = jnp.concatenate(tiles, axis=0).astype(BF16).reshape(2, 8, 16, 128)
        for rel in range(2):
            side = zl if rel == 0 else 1 - zl
            src, dst = CS.at[block, side], CH.at[head, side, pair]
            target = dev(zh_=place(zh, zl, pair, side), x_=block)
            slot = S_CTX + rel * 4 + d
            if d:
                ctx[rel, d] = rcopy(src, dst, slot, target)
                ctx[rel, d].start()
            else:
                local[rel] = pltpu.make_async_copy(src, dst, lsem.at[3 + rel])
                if rel == 0:
                    local[0].start()
                else:
                    ctx[1, 0] = rcopy(src, dst, slot, zhpart)
                    pl.when(pair == 1)(ctx[1, 0].start)
                    pl.when(pair == 0)(local[1].start)
    wait(fetch_o)
    for d in (2, 1, 3):
        for rel in range(2):
            ctx[rel, d].wait_recv()
    local[0].wait()
    pl.when(pair == 1)(ctx[1, 0].wait_recv)
    pl.when(pair == 0)(local[1].wait)

    def out_projection(side, i):
        @pl.loop(i * 4, i * 4 + 4)
        def _(n):
            lhs = jnp.concatenate([CH[hd, side].reshape(256, 128) for hd in range(2)], axis=1)
            span = pl.ds(pl.multiple_of(n * 512, 512), 512)
            PT[rows(side * 256, 256), span] = jnp.dot(lhs, wo[:, span], preferred_element_type=F32).astype(BF16)

    def add_attended(h, sums):
        part = slice(h * 16, (h + 1) * 16)
        own[part, :] = (own[part, :] + sums).astype(BF16).astype(F32)
        piece(G, zl, h, c, y)[...] = normalize(own[part, :], gain2[...])

    scatter(out_projection, add_attended)

    def units(side, n):
        lhs = G[rows(side * 256, 256), :]
        span = rows(n * 256, 256)
        dims = (((1,), (1,)), ((), ()))
        gate = lax.dot_general(lhs, wg[0, span, :], dims, preferred_element_type=F32)
        up = lax.dot_general(lhs, wg[1, span, :], dims, preferred_element_type=F32)
        ACT[rows(side * 256, 256), pl.ds(pl.multiple_of(n * 256, 256), 256)] = (
            gate / (1.0 + jnp.exp(-gate)) * up).astype(BF16)

    def unmix(out):
        @pl.loop(0, D // 128)
        def _(n):
            lane = pl.ds(pl.multiple_of(n * 128, 128), 128)
            for col in range(4):
                mix[pl.ds(col, 8, stride=4), :] = own[col * 8:(col + 1) * 8, lane]
            for i in range(8):
                out[i, :, lane] = mix[i * 4:(i + 1) * 4, :].astype(BF16)

    wait(fetch_g)
    gather([functools.partial(units, zl, n) for n in range(3)])

    unmix(state)

    @pl.loop(0, 3)
    def _(n):
        units(1 - zl, n)

    wait(fetch_d)

    def down_projection(side, i):
        @pl.loop(i * 4, i * 4 + 4)
        def _(n):
            span = pl.ds(pl.multiple_of(n * 512, 512), 512)
            PT[rows(side * 256, 256), span] = jnp.dot(
                ACT[rows(side * 256, 256), :], wd[:, span], preferred_element_type=F32).astype(BF16)

    def add_feed(h, sums):
        part = slice(h * 16, (h + 1) * 16)
        own[part, :] = own[part, :] + sums

    scatter(down_projection, add_feed)
    unmix(result)
    for cp in [*bias_copies.values(), *xc.values(), *zc.values()]:
        cp.wait_send()
    for key, cp in ctx.items():
        if key != (1, 0):
            cp.wait_send()

    @pl.when(pair == 1)
    def _():
        for cp in [*zq.values(), ctx[1, 0]]:
            cp.wait_send()


def shards(cells, norm1_gain, w_qkv, row_bias, w_out, norm2_gain, w_gate_up, w_down):
    vmem = pl.BlockSpec(memory_space=pltpu.VMEM)
    hbm = pl.BlockSpec(memory_space=pl.ANY)
    out = jax.ShapeDtypeStruct(cells.shape, BF16)
    return tuple(pl.pallas_call(
        layer,
        out_shape=(out, out),
        in_specs=[vmem, vmem, hbm, hbm, hbm, vmem, hbm, hbm],
        out_specs=(vmem, vmem),
        scratch_shapes=[
            pltpu.VMEM((3, D, 256), BF16),
            pltpu.VMEM((256, D), BF16),
            pltpu.VMEM((2, UPAD, D), BF16),
            pltpu.VMEM((UPAD, D), BF16),
            pltpu.VMEM((32, 128), F32),
            pltpu.VMEM((32, D), F32),
            pltpu.VMEM((512, D), BF16),
            pltpu.VMEM((512, D), BF16),
            pltpu.VMEM((2, 2, 4, 16, D), BF16),
            pltpu.VMEM((2, 4, 16, D), BF16),
            pltpu.VMEM((2, 2, 16, D), BF16),
            pltpu.VMEM((2, 2, 16, D // 2), BF16),
            pltpu.VMEM((4, 128, 1024), F32),
            pltpu.VMEM((2, 4, 128, 384), BF16),
            pltpu.VMEM((2, 4, 2, 128, 384), BF16),
            pltpu.VMEM((4, 2, 8, 16, 128), BF16),
            pltpu.VMEM((2, 2, 2, 8, 16, 128), BF16),
            pltpu.VMEM((512, UPAD), BF16),
            pltpu.SemaphoreType.DMA((N_SEM,)),
            pltpu.SemaphoreType.DMA((N_SEM,)),
            pltpu.SemaphoreType.DMA((36,)),
        ],
        compiler_params=pltpu.CompilerParams(
            collective_id=0, has_side_effects=True, vmem_limit_bytes=60 * 2**20),
        name="layer",
    )(cells, norm1_gain.reshape(1, D), w_qkv.transpose(1, 0, 2), row_bias, w_out,
      norm2_gain.reshape(1, D), w_gate_up.transpose(1, 2, 0), w_down))


def solution(mesh):
    in_specs = (
        P(("row", "tensor"), None, None),
        P(),
        P(None, None, "tensor"),
        P("tensor", "row", None),
        P("tensor", None),
        P(),
        P(None, None, "tensor"),
        P("tensor", None),
    )
    out_specs = (P(("row", "tensor"), None, None), P(("row", "tensor"), None, None))
    return jax.shard_map(shards, mesh=mesh, in_specs=in_specs, out_specs=out_specs, check_vma=False)
```

```python
import functools
import math

import jax
import jax.numpy as jnp
from jax import lax
from jax.experimental import pallas as pl
from jax.experimental.pallas import tpu as pltpu
from jax.sharding import PartitionSpec as P

MESH = pl.DeviceIdType.MESH
F32 = jnp.float32
BF16 = jnp.bfloat16
D = 4096
UNITS = 688
UPAD = 768
SCALE = 1.0 / math.sqrt(128)

S_BIAS, S_X, S_ZH, S_ZQ, S_CTX = 0, 3, 9, 17, 21
AG_Z, AG_Y, AG_FWD, AG_OWN, AG_NEAR, AG_FAR = 29, 43, 51, 55, 57, 69
RS_C, RS_Z, RS_Y, RS_FWD = 83, 115, 131, 139
N_SEM = 143


def rows(start, count):
    return pl.ds(pl.multiple_of(start, 16), count)


def normalize(values, gain):
    wide = values.astype(F32)
    inverse = lax.rsqrt(jnp.mean(wide * wide, axis=-1, keepdims=True) + 1e-05)
    return (wide * inverse * gain).astype(BF16)


def layer(cells, gain1, wqkv_hbm, bias_hbm, wout_hbm, gain2, wgu_hbm, wdown_hbm, state, result,
          wq, wo, wg, wd, mix, own, G, PT, RC, RZ, RY, RF, BV, QB, XR, CS, CH, ACT, ssem, rsem, lsem):
    r = lax.axis_index("row")
    t = lax.axis_index("tensor")
    zh, x = r // 4, lax.rem(r, 4)
    k, c = t // 2, lax.rem(t, 2)
    zl, y = k // 4, lax.rem(k, 4)

    def m4(v):
        return lax.rem(v + 4, 4)

    def role(x_):
        turn = m4(x_ + c)
        return turn // 2, lax.rem(turn, 2)

    head, pair = role(x)

    def dev(zh_=zh, x_=x, zl_=zl, y_=y, c_=c):
        return (zh_ * 4 + x_, zl_ * 8 + y_ * 2 + c_)

    sib = dev(c_=1 - c)
    zdev = (dev(zl_=1 - zl), dev(zh_=1 - zh, zl_=1 - zl))
    ydev = {d: dev(y_=m4(y + d)) for d in (1, 2, 3)}
    xdev = {d: dev(x_=m4(x + d)) for d in (1, 2, 3)}
    zhpart = dev(zh_=1 - zh)

    def piece(ref, zl_, h, c_, y_):
        return ref.at[rows((zl_ * 16 + h * 8 + c_ * 4 + y_) * 16, 16)]

    def rcopy(src, dst, slot, target):
        return pltpu.make_async_remote_copy(
            src_ref=src, dst_ref=dst, send_sem=ssem.at[slot], recv_sem=rsem.at[slot],
            device_id=target, device_id_type=MESH)

    def fetch(pairs, slot):
        return [pltpu.make_async_copy(src, dst, lsem.at[slot + i]) for i, (src, dst) in enumerate(pairs)]

    own_bias = pltpu.make_async_copy(bias_hbm.at[head], BV.at[x], lsem.at[0])
    fetch_q = fetch([(wqkv_hbm.at[j, pl.ds(i * 1024, 1024)], wq.at[j, pl.ds(i * 1024, 1024)])
                     for j in range(3) for i in range(4)], 8)
    fetch_o = fetch([(wout_hbm.at[pl.ds(i * 64, 64)], wo.at[pl.ds(i * 64, 64)]) for i in range(4)], 20)
    fetch_g = fetch([(wgu_hbm.at[j, pl.ds(i * 176, w)], wg.at[j, pl.ds(i * 176, w)])
                     for i, w in enumerate((176, 176, 176, 160)) for j in range(2)], 24)
    fetch_d = fetch([(wdown_hbm.at[pl.ds(i * 176, w)], wd.at[pl.ds(i * 176, w)])
                     for i, w in enumerate((176, 176, 176, 160))], 32)

    def start(copies):
        for cp in copies:
            cp.start()

    def wait(copies):
        for cp in copies:
            cp.wait()

    start(fetch_q)

    barrier = pltpu.get_barrier_semaphore()
    peers = [sib, zdev[0], zdev[1], zhpart] + [ydev[d] for d in (1, 2, 3)] + [xdev[d] for d in (1, 2, 3)]
    peers += [dev(zh_=1 - zh, x_=m4(x + d)) for d in (1, 2, 3)]
    for target in peers:
        pl.semaphore_signal(barrier, inc=1, device_id=target, device_id_type=MESH)

    @pl.loop(0, D // 128)
    def _(n):
        lane = pl.ds(pl.multiple_of(n * 128, 128), 128)
        for i in range(8):
            mix[i * 4:(i + 1) * 4, :] = cells[i, :, lane].astype(F32)
        for col in range(4):
            own[col * 8:(col + 1) * 8, lane] = mix[pl.ds(col, 8, stride=4), :]

    for h in range(2):
        piece(G, zl, h, c, y)[...] = normalize(own[h * 16:(h + 1) * 16, :], gain1[...])

    pl.semaphore_wait(barrier, len(peers))

    lanes = (pl.ds(0, D // 2), pl.ds(D // 2, D // 2))
    turns = ((0, 1), (1, 3), (1, 1), (0, 3))

    def first(d):
        return d // 2

    def gather(middle):
        sends = []

        def send(ref, slot, target):
            cp = rcopy(ref, ref, slot, target)
            cp.start()
            sends.append(cp)
            return cp

        zs, ys, fwd, near, far = {}, {}, {}, [], []
        steps = [(h, d, first(d)) for h, d in turns] + [(h, d, 1 - first(d)) for h, d in turns]
        ahead = [(h, 2, first(d)) for h, d in turns]

        def own(h):
            return piece(G, zl, h, c, y)

        def hop(h, d, i):
            ys[h, d, i] = send(own(h).at[:, lanes[i]], AG_Y + h * 4 + first(d) * 2 + i, ydev[d])

        def spot(zl_, h, d, i):
            return piece(G, zl_, h, c, m4(y - d)).at[:, lanes[i]]

        def spread(h, d, i):
            src = spot(zl, h, d, i)
            zs[h, d, i] = send(src, AG_Z + h * 7 + d * 2 + i - 1, zdev[h])
            near.append(send(src, AG_NEAR + h * 6 + d * 2 + i - 2, sib))

        def arrive(h, d, i):
            ys[h, d, i].wait_recv()
            if i == first(d):
                fwd[h, i] = send(spot(zl, h, d, i), AG_FWD + h * 2 + i, ydev[d])
            spread(h, d, i)

        def cross(h, d, i):
            zs[h, d, i].wait_recv()
            far.append(send(spot(1 - zl, h, d, i), AG_FAR + h * 7 + d * 2 + i - 1, sib))

        for step in steps[:4]:
            hop(*step)
        for h in range(2):
            zs[h, 0] = send(own(h), AG_Z + h * 7, zdev[h])
        for step in steps[4:]:
            hop(*step)
        for h in range(2):
            near.append(send(own(h), AG_OWN + h, sib))
        for step in steps[:4]:
            arrive(*step)
        for h in range(2):
            zs[h, 0].wait_recv()
            far.append(send(piece(G, 1 - zl, h, c, y), AG_FAR + h * 7, sib))
        for step in steps[4:]:
            arrive(*step)
        for step in steps[:4]:
            cross(*step)
        for h, d, i in ahead:
            fwd[h, i].wait_recv()
            spread(h, d, i)
        for cp in near:
            cp.wait_recv()
        middle[0]()
        for step in steps[4:]:
            cross(*step)
        middle[1]()
        for step in ahead:
            cross(*step)
        middle[2]()
        for cp in far:
            cp.wait_recv()
        for cp in sends:
            cp.wait_send()

    def scatter(produce, finish):
        sends = []

        def send(src, dst, slot, target):
            cp = rcopy(src, dst, slot, target)
            cp.start()
            sends.append(cp)
            return cp

        def add(slot, *others):
            total = slot[...].astype(F32)
            for other in others:
                total = total + other[...].astype(F32)
            slot[...] = total.astype(BF16)

        order = [(0, 2), (1, 2), *turns, (0, 0), (1, 0)]
        cs, zs, ys, fwd = {}, {}, {}, {}

        def share(zrel):
            side = zl if zrel == 0 else 1 - zl
            for i in range(2):
                produce(side, i)
                for h, d in order:
                    cs[h, d, i] = send(piece(PT, side, h, 1 - c, m4(y + d)).at[:, lanes[i]],
                                       RC.at[zrel, h, d, :, lanes[i]], RS_C + zrel * 16 + h * 8 + d * 2 + i, sib)

        def pair_up(zrel, h, d, i):
            cs[h, d, i].wait_recv()
            side = zl if zrel == 0 else 1 - zl
            add(RC.at[zrel, h, d, :, lanes[i]], piece(PT, side, h, c, m4(y + d)).at[:, lanes[i]])

        def cross(h, d, i):
            pair_up(1, h, d, i)
            zs[h, d, i] = send(RC.at[1, h, d, :, lanes[i]], RZ.at[h, d, :, lanes[i]],
                               RS_Z + h * 8 + d * 2 + i, zdev[h])

        def hop(h, d, i, *others):
            pair_up(0, h, d, i)
            zs[h, d, i].wait_recv()
            slot = RC.at[0, h, d, :, lanes[i]]
            add(slot, RZ.at[h, d, :, lanes[i]], *others)
            ys[h, d, i] = send(slot, RY.at[h, first(d), :, lanes[i]], RS_Y + h * 4 + first(d) * 2 + i, ydev[d])

        share(1)
        for i, d in ((0, 3), (1, 1)):
            for h in range(2):
                cross(h, 2, i)
            for h in range(2):
                cross(h, d, i)
        for h, d in turns:
            cross(h, d, first(d))
        for h in range(2):
            for i in range(2):
                cross(h, 0, i)
        share(0)
        for i, d in ((0, 1), (1, 3)):
            for h in range(2):
                pair_up(0, h, 2, i)
                zs[h, 2, i].wait_recv()
                slot = RC.at[0, h, 2, :, lanes[i]]
                add(slot, RZ.at[h, 2, :, lanes[i]])
                fwd[h, i] = send(slot, RF.at[h, i], RS_FWD + h * 2 + i, ydev[d])
        for h, d in turns:
            hop(h, d, 1 - first(d))
        for h, d in turns:
            fwd[h, first(d)].wait_recv()
            hop(h, d, first(d), RF.at[h, first(d)])
        for h in range(2):
            for i in range(2):
                pair_up(0, h, 0, i)
        for h in range(2):
            for i in range(2):
                zs[h, 0, i].wait_recv()
            sums = RC[0, h, 0].astype(F32) + RZ[h, 0].astype(F32)
            for d in (1, 3):
                for i in range(2):
                    ys[h, d, i].wait_recv()
                sums = sums + RY[h, first(d)].astype(F32)
            finish(h, sums)
        for cp in sends:
            cp.wait_send()

    own_bias.start()
    bias_copies = {d: rcopy(bias_hbm.at[role(m4(x + d))[0]], BV.at[x], S_BIAS + d - 1, xdev[d]) for d in (1, 2, 3)}
    for d in (1, 3):
        bias_copies[d].start()

    xc, own_x = {}, {}

    def place(zh_, zl_, pair_, part):
        return zh_ + pair_ * lax.rem(zl_ + part, 2) * (1 - 2 * zh_)

    def project(side, j):
        lhs = G[rows(side * 256, 256), :]
        acc = jnp.dot(lhs, wq[j], preferred_element_type=F32).reshape(2, 2, 4, 2, 8, 256)
        for h in range(2):
            for col in range(2):
                tiles = [acc[h, cc, yy, col] for yy in range(4) for cc in range(2)]
                val = jnp.concatenate(tiles, axis=0).astype(BF16)
                for hd in range(2):
                    QB[hd, h * 2 + col, rows(side * 64, 64), j * 128:(j + 1) * 128] = val[:, hd * 128:(hd + 1) * 128]

    def ship(side, rel):
        part = rows(side * 64, 64)
        for d in (2, 1, 3, 0):
            head_, pair_ = role(m4(x + d))
            src = QB.at[head_, pl.ds(pair_ * 2, 2), part]
            dst = XR.at[place(zh, zl, pair_, side), x, :, part]
            if d:
                xc[rel, d] = rcopy(src, dst, S_X + rel * 3 + d - 1, xdev[d])
                xc[rel, d].start()
            else:
                own_x[rel] = pltpu.make_async_copy(src, dst, lsem.at[1 + rel])
                own_x[rel].start()

    def last_step():
        project(zl, 2)
        ship(zl, 0)
        start(fetch_o)
        start(fetch_g)
        start(fetch_d)

    wait(fetch_q)
    gather([functools.partial(project, zl, 0), functools.partial(project, zl, 1), last_step])

    zc, zq = {}, {}

    def pass_on(side, rel):
        part = rows(side * 64, 64)
        for d in (0, 1, 3, 2):
            if d:
                xc[rel, d].wait_recv()
            else:
                own_x[rel].wait()
            spot = (place(zh, zl, pair, side), m4(x - d), slice(None), part)
            if rel:
                ref = XR.at[spot + (pl.ds(0, 128),)]
                zq[d] = rcopy(ref, ref, S_ZQ + d, zhpart)
                pl.when(pair == 1)(zq[d].start)
            ref = XR.at[spot + (pl.ds(128, 256),)]
            zc[rel, d] = rcopy(ref, ref, S_ZH + rel * 4 + d, zhpart)
            zc[rel, d].start()

    for j in range(3):
        project(1 - zl, j)
    ship(1 - zl, 1)
    bias_copies[2].start()
    pass_on(zl, 0)
    pass_on(1 - zl, 1)
    wg[:, UNITS:UPAD, :] = jnp.zeros((2, UPAD - UNITS, D), BF16)
    wd[UNITS:UPAD, :] = jnp.zeros((UPAD - UNITS, D), BF16)
    own_bias.wait()
    for d in (1, 3):
        bias_copies[d].wait_recv()
    for cp in zc.values():
        cp.wait_recv()
    for cp in zq.values():
        pl.when(pair == 1)(cp.wait_recv)

    ctx = {}
    local = {}
    for d in (1, 3, 0, 2):
        block = m4(x + d)
        heads_out = []
        if d == 2:
            bias_copies[2].wait_recv()
        for col in range(2):
            q = XR[zh, block, col, :, 0:128]
            k1 = XR[0, :, col, :, 128:256].reshape(512, 128)
            k2 = XR[1, :, col, :, 128:256].reshape(512, 128)
            dims = (((1,), (1,)), ((), ()))
            s1 = lax.dot_general(q, k1, dims, preferred_element_type=F32) * SCALE + BV[block, :, 0:512]
            s2 = lax.dot_general(q, k2, dims, preferred_element_type=F32) * SCALE + BV[block, :, 512:1024]
            peak = jnp.maximum(jnp.max(s1, axis=-1, keepdims=True), jnp.max(s2, axis=-1, keepdims=True))
            e1, e2 = jnp.exp(s1 - peak), jnp.exp(s2 - peak)
            total = jnp.sum(e1, axis=-1, keepdims=True) + jnp.sum(e2, axis=-1, keepdims=True)
            v1 = XR[0, :, col, :, 256:384].reshape(512, 128)
            v2 = XR[1, :, col, :, 256:384].reshape(512, 128)
            out = jnp.dot(e1.astype(BF16), v1, preferred_element_type=F32)
            out = out + jnp.dot(e2.astype(BF16), v2, preferred_element_type=F32)
            heads_out.append((out / total).reshape(2, 4, 2, 8, 128))
        tiles = [heads_out[col][zz, yy, cc] for zz in range(2) for cc in range(2) for yy in range(4) for col in range(2)]
        CS[block] = jnp.concatenate(tiles, axis=0).astype(BF16).reshape(2, 8, 16, 128)
        for rel in range(2):
            side = zl if rel == 0 else 1 - zl
            src, dst = CS.at[block, side], CH.at[head, side, pair]
            target = dev(zh_=place(zh, zl, pair, side), x_=block)
            slot = S_CTX + rel * 4 + d
            if d:
                ctx[rel, d] = rcopy(src, dst, slot, target)
                ctx[rel, d].start()
            else:
                local[rel] = pltpu.make_async_copy(src, dst, lsem.at[3 + rel])
                if rel == 0:
                    local[0].start()
                else:
                    ctx[1, 0] = rcopy(src, dst, slot, zhpart)
                    pl.when(pair == 1)(ctx[1, 0].start)
                    pl.when(pair == 0)(local[1].start)
    wait(fetch_o)
    for d in (2, 1, 3):
        for rel in range(2):
            ctx[rel, d].wait_recv()
    local[0].wait()
    pl.when(pair == 1)(ctx[1, 0].wait_recv)
    pl.when(pair == 0)(local[1].wait)

    def out_projection(side, i):
        @pl.loop(i * 4, i * 4 + 4)
        def _(n):
            lhs = jnp.concatenate([CH[hd, side].reshape(256, 128) for hd in range(2)], axis=1)
            span = pl.ds(pl.multiple_of(n * 512, 512), 512)
            PT[rows(side * 256, 256), span] = jnp.dot(lhs, wo[:, span], preferred_element_type=F32).astype(BF16)

    def add_attended(h, sums):
        part = slice(h * 16, (h + 1) * 16)
        own[part, :] = (own[part, :] + sums).astype(BF16).astype(F32)
        piece(G, zl, h, c, y)[...] = normalize(own[part, :], gain2[...])

    scatter(out_projection, add_attended)

    def units(side, n):
        lhs = G[rows(side * 256, 256), :]
        span = rows(n * 256, 256)
        dims = (((1,), (1,)), ((), ()))
        gate = lax.dot_general(lhs, wg[0, span, :], dims, preferred_element_type=F32)
        up = lax.dot_general(lhs, wg[1, span, :], dims, preferred_element_type=F32)
        ACT[rows(side * 256, 256), pl.ds(pl.multiple_of(n * 256, 256), 256)] = (
            gate / (1.0 + jnp.exp(-gate)) * up).astype(BF16)

    wait(fetch_g)
    gather([functools.partial(units, zl, n) for n in range(3)])

    state[...] = own[...].astype(BF16)

    @pl.loop(0, 3)
    def _(n):
        units(1 - zl, n)

    wait(fetch_d)

    def down_projection(side, i):
        @pl.loop(i * 4, i * 4 + 4)
        def _(n):
            span = pl.ds(pl.multiple_of(n * 512, 512), 512)
            PT[rows(side * 256, 256), span] = jnp.dot(
                ACT[rows(side * 256, 256), :], wd[:, span], preferred_element_type=F32).astype(BF16)

    def add_feed(h, sums):
        part = slice(h * 16, (h + 1) * 16)
        result[part, :] = (own[part, :] + sums).astype(BF16)

    scatter(down_projection, add_feed)
    for cp in [*bias_copies.values(), *xc.values(), *zc.values()]:
        cp.wait_send()
    for key, cp in ctx.items():
        if key != (1, 0):
            cp.wait_send()

    @pl.when(pair == 1)
    def _():
        for cp in [*zq.values(), ctx[1, 0]]:
            cp.wait_send()


def shards(cells, norm1_gain, w_qkv, row_bias, w_out, norm2_gain, w_gate_up, w_down):
    vmem = pl.BlockSpec(memory_space=pltpu.VMEM)
    hbm = pl.BlockSpec(memory_space=pl.ANY)
    out = jax.ShapeDtypeStruct((32, D), BF16)
    state, result = pl.pallas_call(
        layer,
        out_shape=(out, out),
        in_specs=[vmem, vmem, hbm, hbm, hbm, vmem, hbm, hbm],
        out_specs=(vmem, vmem),
        scratch_shapes=[
            pltpu.VMEM((3, D, 256), BF16),
            pltpu.VMEM((256, D), BF16),
            pltpu.VMEM((2, UPAD, D), BF16),
            pltpu.VMEM((UPAD, D), BF16),
            pltpu.VMEM((32, 128), F32),
            pltpu.VMEM((32, D), F32),
            pltpu.VMEM((512, D), BF16),
            pltpu.VMEM((512, D), BF16),
            pltpu.VMEM((2, 2, 4, 16, D), BF16),
            pltpu.VMEM((2, 4, 16, D), BF16),
            pltpu.VMEM((2, 2, 16, D), BF16),
            pltpu.VMEM((2, 2, 16, D // 2), BF16),
            pltpu.VMEM((4, 128, 1024), F32),
            pltpu.VMEM((2, 4, 128, 384), BF16),
            pltpu.VMEM((2, 4, 2, 128, 384), BF16),
            pltpu.VMEM((4, 2, 8, 16, 128), BF16),
            pltpu.VMEM((2, 2, 2, 8, 16, 128), BF16),
            pltpu.VMEM((512, UPAD), BF16),
            pltpu.SemaphoreType.DMA((N_SEM,)),
            pltpu.SemaphoreType.DMA((N_SEM,)),
            pltpu.SemaphoreType.DMA((36,)),
        ],
        compiler_params=pltpu.CompilerParams(
            collective_id=0, has_side_effects=True, vmem_limit_bytes=60 * 2**20),
        name="layer",
    )(cells, norm1_gain.reshape(1, D), w_qkv.transpose(1, 0, 2), row_bias, w_out,
      norm2_gain.reshape(1, D), w_gate_up.transpose(1, 2, 0), w_down)
    return tuple(v.reshape(4, 8, D).transpose(1, 0, 2) for v in (state, result))


def solution(mesh):
    in_specs = (
        P(("row", "tensor"), None, None),
        P(),
        P(None, None, "tensor"),
        P("tensor", "row", None),
        P("tensor", None),
        P(),
        P(None, None, "tensor"),
        P("tensor", None),
    )
    out_specs = (P(("row", "tensor"), None, None), P(("row", "tensor"), None, None))
    return jax.shard_map(shards, mesh=mesh, in_specs=in_specs, out_specs=out_specs, check_vma=False)
```
